256 devices in a mesh: seq: 32 (over z, y_lo, core), head: 8 (over y_hi, x).
Axes of the slice: x: 4, y: 4 (y_hi: 2, y_lo: 2; y = y_hi * 2 + y_lo), z: 8, core: 2. Of those that a mesh axis runs over, the one named last changes fastest.
Arguments:
- queries: bfloat16 [32768, 4096], P('seq', 'head'), may hold values from -6 to 6
- keys: bfloat16 [32768, 4096], P('seq', 'head'), may hold values from -6 to 6
- values: bfloat16 [32768, 4096], P('seq', 'head'), may hold values from -6 to 6
- out_weight: bfloat16 [4096, 4096], P('head'), may hold values from -1.5 to 1.5
Outputs:
- mixed: bfloat16 [32768, 4096], P('seq', 'head')
The draws below stay inside these ranges and needn't reach their ends.
All inputs are finite; a program needn't handle non-finite values.
Results may differ from the reference program's by a relative error of at most 0.015.
Values may be sent and summed in bfloat16 or wider, within the bound.
A program may use at most 192 MiB of HBM per device.

```python
import math
import jax
import jax.numpy as jnp
from jax import lax

HEADS = 32
HEAD_DIM = 128
D = 4096
TOKENS = 32768
SEG1 = 2048
SEG2 = 8192
N_HEAD = 8


def draw_queries(key, part):
    drawn = 1.5 * jnp.clip(jax.random.normal(jax.random.fold_in(key, 11), (TOKENS, D), jnp.float32), -4.0, 4.0)
    return drawn.astype(jnp.bfloat16)


def draw_keys(key, part):
    drawn = jnp.clip(jax.random.normal(jax.random.fold_in(key, 12), (TOKENS, D), jnp.float32), -6.0, 6.0)
    return drawn.astype(jnp.bfloat16)


def block_scale(own_key, shape, shards, smallest, top_value):
    level = 1.0
    for dim, shards_of in shards:
        draws = jax.random.uniform(jax.random.fold_in(jax.random.fold_in(own_key, 6), dim), (shards_of,), jnp.float32, smallest / len(shards), top_value / len(shards))
        level = level * jnp.repeat(jnp.exp(draws), shape[dim] // shards_of).reshape((-1,) + (1,) * (len(shape) - 1 - dim))
    return level


def gaussian(key, shape, scale, limit, split=(), kind=jnp.bfloat16):
    entries = jax.random.normal(key, shape, jnp.float32) * scale
    if len(split) > 0:
        entries = block_scale(key, shape, split, -0.22, 0.18) * entries
    return jnp.clip(entries, min=-limit, max=limit).astype(kind)


def setup_inputs(seed: int = 0) -> dict:
    splits = jax.random.split(jax.random.key(seed), 5)
    queries = draw_queries(jax.random.fold_in(splits[4], 71), 0)
    keys = draw_keys(jax.random.fold_in(splits[4], 71), 0)
    values = gaussian(splits[2], (TOKENS, D), 1.0, 6.0, ((0, 32), (1, 8)))
    out_weight = gaussian(splits[3], (D, D), 0.25, 1.5, ((0, 8),))
    return {"queries": queries, "keys": keys, "values": values, "out_weight": out_weight}


NEG_FILL = -1e+30

def causal_level(query, key_rows, value_rows, seg_len, scale):
    count = query.shape[0] // seg_len
    lower = jnp.arange(seg_len)[:, None] >= jnp.arange(seg_len)[None, :]

    def one_segment(parts):
        seg_query, seg_keys, seg_values = parts
        scores = jnp.dot(seg_query, seg_keys.T, preferred_element_type=jnp.float32) * scale
        scores = jnp.where(lower, scores, NEG_FILL)
        peak = lax.optimization_barrier(jnp.max(scores, axis=1))
        weights = jnp.where(lower, jnp.exp(scores - peak[:, None]), 0.0)
        total = lax.optimization_barrier(jnp.sum(weights, axis=1))
        numer = jnp.dot(weights.astype(jnp.bfloat16), seg_values, preferred_element_type=jnp.float32)
        return (numer, peak, total)
    numer, peak, total = lax.map(one_segment, (query.reshape(count, seg_len, -1), key_rows.reshape(count, seg_len, -1), value_rows.reshape(count, seg_len, -1)))
    return (numer.reshape(-1, numer.shape[-1]), peak.reshape(-1), total.reshape(-1))

def dilated(source, stride, offset):
    shaped = source.reshape(-1, stride, source.shape[1])
    return lax.dynamic_index_in_dim(shaped, offset, axis=1, keepdims=False)

def spread_level(state, stride, offset):
    numer, peak, total = state
    picker = jnp.arange(stride, dtype=jnp.int32) == offset
    numer_full = jnp.where(picker[None, :, None], numer[:, None, :], 0.0).reshape(-1, numer.shape[-1])
    peak_full = jnp.where(picker[None, :], peak[:, None], NEG_FILL).reshape(-1)
    total_full = jnp.where(picker[None, :], total[:, None], 0.0).reshape(-1)
    return (numer_full, peak_full, total_full)

def reference(queries, keys, values, out_weight):
    scale = 1.0 / math.sqrt(HEAD_DIM)

    def one_head(head_id):
        column = head_id * HEAD_DIM
        head_query = lax.dynamic_slice_in_dim(queries, column, HEAD_DIM, 1)
        head_keys = lax.dynamic_slice_in_dim(keys, column, HEAD_DIM, 1)
        head_values = lax.dynamic_slice_in_dim(values, column, HEAD_DIM, 1)
        near = causal_level(head_query, head_keys, head_values, SEG1, scale)
        mid_off = head_id % 4
        middle = causal_level(dilated(head_query, 4, mid_off), dilated(head_keys, 4, mid_off), dilated(head_values, 4, mid_off), SEG2 // 4, scale)
        middle = spread_level(middle, 4, mid_off)
        far_off = head_id % 16
        far = causal_level(dilated(head_query, 16, far_off), dilated(head_keys, 16, far_off), dilated(head_values, 16, far_off), TOKENS // 16, scale)
        far = spread_level(far, 16, far_off)
        top = jnp.maximum(jnp.maximum(near[1], middle[1]), far[1])
        numer = jnp.zeros_like(near[0])
        total = jnp.zeros_like(near[2])
        for level in (near, middle, far):
            factor = jnp.exp(level[1] - top)
            numer = numer + level[0] * factor[:, None]
            total = total + level[2] * factor
        return (numer / total[:, None]).astype(jnp.bfloat16)
    heads_out = lax.map(one_head, jnp.arange(HEADS, dtype=jnp.int32))
    attended = jnp.transpose(heads_out, (1, 0, 2)).reshape(TOKENS, D)
    group_cols = D // N_HEAD
    summed = jnp.zeros((TOKENS, D), jnp.float32)
    for group in range(N_HEAD):
        partial_sum = jnp.dot(attended[:, group * group_cols:(group + 1) * group_cols], out_weight[group * group_cols:(group + 1) * group_cols, :], preferred_element_type=jnp.float32)
        rounded = lax.optimization_barrier(partial_sum.astype(jnp.bfloat16))
        summed = summed + rounded.astype(jnp.float32)
    return summed.astype(jnp.bfloat16)
```

```python
import functools
import math

import jax
import jax.numpy as jnp
from jax import lax
from jax.experimental import pallas as pl
from jax.experimental.pallas import tpu as pltpu
from jax.sharding import PartitionSpec as P

DH = 128
ROWS = 1024
HEADS = 4
TILE = 256
NEG = -1e30
SCALE2 = math.log2(math.e) / math.sqrt(DH)
MESH = pl.DeviceIdType.MESH
bf16 = jnp.bfloat16
f32 = jnp.float32


def nt_dot(a, b):
    return lax.dot_general(a, b, (((1,), (1,)), ((), ())), preferred_element_type=f32)


def softmax_pieces(query, pieces):
    scores = []
    for key_rows, _, limit in pieces:
        score = nt_dot(query, key_rows)
        if limit is not None:
            row = lax.broadcasted_iota(jnp.int32, score.shape, 0)
            col = lax.broadcasted_iota(jnp.int32, score.shape, 1)
            score = jnp.where(col - row <= limit, score, NEG)
        scores.append(score)
    peak = functools.reduce(jnp.maximum, [jnp.max(s, axis=1, keepdims=True) for s in scores])
    both = None
    for score, (_, value_rows, _) in zip(scores, pieces):
        weights = jnp.exp2((score - peak) * SCALE2).astype(bf16)
        ones = jnp.ones(value_rows.shape, bf16)
        term = jnp.dot(weights, jnp.concatenate([value_rows, ones], axis=1), preferred_element_type=f32)
        both = term if both is None else both + term
    numer, total = both[:, :DH], both[:, DH:]
    return numer, jnp.broadcast_to(peak, numer.shape), total


def merge(one, two):
    numer1, peak1, total1 = one
    numer2, peak2, total2 = two
    top = jnp.maximum(peak1, peak2)
    f1 = jnp.exp2((peak1 - top) * SCALE2)
    f2 = jnp.exp2((peak2 - top) * SCALE2)
    return numer1 * f1 + numer2 * f2, top, total1 * f1 + total2 * f2


def attend_kernel(
    planes,
    q_hbm, k_hbm, v_hbm, w_hbm, att_ref, wg_ref,
    QA, KV, SM, SF, FQ, FKV, ACC, PK, TT, TMP, RO, RST, OB, ST,
    loc, locw, w_ss, w_rs, wf_ss, wf_rs, n_ss, n_rs, p_ss, p_rs, pv_ss, pv_rs,
    f_ss, f_rs, b_ss, b_rs, r_ss, r_rs,
):
    seq = lax.axis_index("seq")
    head = lax.axis_index("head")
    z = seq // 4
    i = seq % 4
    core = seq % 2
    zpar = z % 2
    x = head % 4
    y = head // 4

    def dev(plane, slot):
        return (plane * 4 + slot, head)

    def plane_peer(d):
        return (i + d) % 4

    pair = z + 1 - 2 * zpar
    znext = (z + 1) % planes
    zprev = (z + planes - 1) % planes
    zother = (z + planes - 1 + 2 * zpar) % planes

    loads = []
    for h in range(HEADS):
        cols = slice(h * DH, (h + 1) * DH)
        loads.append([
            pltpu.make_async_copy(q_hbm.at[:, cols], QA.at[h], loc.at[h, 0]),
            pltpu.make_async_copy(k_hbm.at[:, cols], KV.at[h, 0, pl.ds(ROWS, ROWS)], loc.at[h, 1]),
            pltpu.make_async_copy(v_hbm.at[:, cols], KV.at[h, 1, pl.ds(ROWS, ROWS)], loc.at[h, 2]),
        ])
        for copy in loads[-1]:
            copy.start()

    barrier = pltpu.get_barrier_semaphore()
    greet = [dev(z, plane_peer(d)) for d in (1, 2, 3)]
    greet += [dev(pair, s) for s in range(4)]
    greet += [dev(zother, i)]
    greet += [(seq, y * 4 + (x + d) % 4) for d in (1, 2, 3)]
    for target in greet:
        pl.semaphore_signal(barrier, inc=1, device_id=target, device_id_type=MESH)
    pl.semaphore_wait(barrier, len(greet))

    def near_copy(h, a):
        src = (k_hbm, v_hbm)[a].at[:, h * DH:(h + 1) * DH]
        return pltpu.make_async_remote_copy(
            src, KV.at[h, a, pl.ds(0, ROWS)], n_ss.at[h, a], n_rs.at[h, a],
            device_id=dev(z, i + 1 - 2 * core), device_id_type=MESH)

    @pl.when(core == 0)
    def _():
        for h in range(HEADS):
            for a in range(2):
                near_copy(h, a).start()

    half = pl.multiple_of(core * 256, 256)

    def w_copy(d, yr):
        xd = (x + d) % 4
        yd = (y + yr) % 2
        col = pl.multiple_of((yd * 4 + xd) * 512, 512)
        return pltpu.make_async_remote_copy(
            w_hbm.at[pl.ds(half, 256), pl.ds(col, 512)],
            wg_ref.at[yr, x, pl.ds(half, 256)],
            w_ss.at[d - 1, yr], w_rs.at[d - 1, yr],
            device_id=(seq, y * 4 + xd), device_id_type=MESH)

    def w_arrived(d, yr):
        xs = (x + 4 - d) % 4
        return pltpu.make_async_remote_copy(
            wg_ref.at[yr, xs, pl.ds(half, 256)],
            wg_ref.at[yr, xs, pl.ds(half, 256)],
            w_ss.at[d - 1, yr], w_rs.at[d - 1, yr],
            device_id=(seq, y * 4 + xs), device_id_type=MESH)

    def w_forward(d, yr):
        xs = (x + 4 - d) % 4
        return pltpu.make_async_remote_copy(
            wg_ref.at[yr, xs, pl.ds(half, 256)],
            wg_ref.at[yr, xs, pl.ds(half, 256)],
            wf_ss.at[d - 1, yr], wf_rs.at[d - 1, yr],
            device_id=dev(z, i + 1 - 2 * core), device_id_type=MESH)

    def w_forwarded(d, yr):
        xs = (x + 4 - d) % 4
        other = pl.multiple_of(256 - half, 256)
        return pltpu.make_async_remote_copy(
            wg_ref.at[yr, xs, pl.ds(other, 256)],
            wg_ref.at[yr, xs, pl.ds(other, 256)],
            wf_ss.at[d - 1, yr], wf_rs.at[d - 1, yr],
            device_id=dev(z, i + 1 - 2 * core), device_id_type=MESH)

    for d in (1, 3, 2):
        for yr in range(2):
            w_copy(d, yr).start()

    def w_own(yr):
        col = pl.multiple_of((((y + yr) % 2) * 4 + x) * 512, 512)
        return pltpu.make_async_copy(w_hbm.at[:, pl.ds(col, 512)], wg_ref.at[yr, x], locw.at[yr])

    for yr in range(2):
        w_own(yr).start()

    for h in range(HEADS):
        for a in range(3):
            loads[h][a].wait()
            source = QA[h] if a == 0 else KV[h, a - 1, ROWS:, :]
            TMP[a] = source.astype(f32)
            SM[h, a] = TMP[a, pl.ds(h, 256, stride=4), :].astype(bf16)
            SF[h, a] = TMP[a, pl.ds(4 * x + h, 64, stride=16), :].astype(bf16)

    def plane_copy(d, kind):
        s = plane_peer(d)
        return plane_descriptor(d, kind, s, i, s)

    def plane_arrived(d, kind):
        s = (i + 4 - d) % 4
        return plane_descriptor(d, kind, s, s, i)

    def plane_descriptor(d, kind, target, sender, slot):
        mid = pl.multiple_of(sender * 256, 256)
        far = pl.multiple_of(sender * 64, 64)
        src, dst = (
            (SF.at[slot, pl.ds(1, 2)], FKV.at[z, :, pl.ds(far, 64)]),
            (SF.at[slot, 0], FQ.at[pl.ds(far, 64)]),
            (SM.at[slot, pl.ds(1, 2)], KV.at[4, :, pl.ds(ROWS + mid, 256)]),
            (SM.at[slot, 0], QA.at[4, pl.ds(mid, 256)]),
        )[kind]
        return pltpu.make_async_remote_copy(
            src, dst, p_ss.at[d - 1, kind], p_rs.at[d - 1, kind],
            device_id=dev(z, target), device_id_type=MESH)

    def prev_copy(s):
        return pltpu.make_async_remote_copy(
            SM.at[s, pl.ds(1, 2)], KV.at[4, :, pl.ds(pl.multiple_of(i * 256, 256), 256)],
            pv_ss.at[s], pv_rs.at[i], device_id=dev(pair, s), device_id_type=MESH)

    def prev_arrived(s):
        return pltpu.make_async_remote_copy(
            SM.at[s, pl.ds(1, 2)], KV.at[4, :, pl.ds(s * 256, 256)],
            pv_ss.at[s], pv_rs.at[s], device_id=dev(pair, s), device_id_type=MESH)

    for kind in (0, 1):
        for d in (2, 3, 1):
            plane_copy(d, kind).start()

    @pl.when(zpar == 0)
    def _():
        for s in range(4):
            prev_copy(s).start()

    for kind in (2, 3):
        for d in (2, 3, 1):
            plane_copy(d, kind).start()

    own_mid = pl.multiple_of(i * 256, 256)
    own_far = pl.multiple_of(i * 64, 64)
    QA[4, pl.ds(own_mid, 256), :] = SM[i, 0]
    FQ[pl.ds(own_far, 64), :] = SF[i, 0]
    for a in range(2):
        KV[4, a, pl.ds(ROWS + own_mid, 256), :] = SM[i, 1 + a]
        FKV[z, a, pl.ds(own_far, 64), :] = SF[i, 1 + a]

    def forward(hop, slot):
        return pltpu.make_async_remote_copy(
            FKV.at[slot], FKV.at[slot], f_ss.at[hop], f_rs.at[hop],
            device_id=dev(znext, i), device_id_type=MESH)

    def backward(hop, slot):
        return pltpu.make_async_remote_copy(
            FKV.at[slot], FKV.at[slot], b_ss.at[hop], b_rs.at[hop],
            device_id=dev(zprev, i), device_id_type=MESH)

    def tiles(h, with_prev):
        for b in range(ROWS // TILE):
            rows = slice(b * TILE, (b + 1) * TILE)
            pieces = []
            if with_prev:
                pieces.append((KV[h, 0, :ROWS, :], KV[h, 1, :ROWS, :], None))
            if b:
                pieces.append((KV[h, 0, ROWS:ROWS + b * TILE, :], KV[h, 1, ROWS:ROWS + b * TILE, :], None))
            diag = slice(ROWS + b * TILE, ROWS + (b + 1) * TILE)
            pieces.append((KV[h, 0, diag, :], KV[h, 1, diag, :], 0))
            numer, peak, total = softmax_pieces(QA[h, rows, :], pieces)
            ACC[h, rows, :] = numer
            PK[h, rows, :] = peak
            TT[h, rows, :] = total

    nfwd = planes // 2
    nbwd = planes - 1 - nfwd

    def level_step(h, carry):
        @pl.when((h < 4) & (core == 1))
        def _():
            for a in range(2):
                pltpu.make_async_remote_copy(
                    KV.at[h, a, pl.ds(0, ROWS)], KV.at[h, a, pl.ds(0, ROWS)], n_ss.at[h, a], n_rs.at[h, a],
                    device_id=dev(z, i + 1 - 2 * core), device_id_type=MESH).wait_recv()

        @pl.when(h == 4)
        def _():
            for kind in (2, 3):
                for d in (1, 2, 3):
                    plane_arrived(d, kind).wait_recv()

            @pl.when(zpar == 1)
            def _():
                for s in range(4):
                    prev_arrived(s).wait_recv()

        parity = jnp.where(h < 4, core, zpar)

        @pl.when(parity == 1)
        def _():
            tiles(h, True)

        @pl.when(parity == 0)
        def _():
            tiles(h, False)

        @pl.when(h == 0)
        def _():
            for kind in (0, 1):
                for d in (1, 2, 3):
                    plane_arrived(d, kind).wait_recv()

        @pl.when((h >= 1) & (h <= nfwd))
        def _():
            forward(h - 1, (z + planes - h) % planes).wait_recv()

        @pl.when((h >= 1) & (h <= nbwd))
        def _():
            backward(h - 1, (z + h) % planes).wait_recv()

        @pl.when(h < nfwd)
        def _():
            forward(h, (z + planes - h) % planes).start()

        @pl.when(h < nbwd)
        def _():
            backward(h, (z + h) % planes).start()

        return carry

    lax.fori_loop(0, HEADS + 1, level_step, 0)

    far_pieces = [(FKV[j, 0], FKV[j, 1], TILE * (z - j)) for j in range(planes)]
    far = softmax_pieces(FQ[...], far_pieces)
    picked = (4, pl.ds(x, 256, stride=4), slice(None))
    mid = (ACC[picked], PK[picked], TT[picked])
    ACC[picked], PK[picked], TT[picked] = merge(mid, far)

    lane = lax.broadcasted_iota(jnp.int32, (256, DH), 1)
    for s in range(4):
        rows = slice(s * 256, (s + 1) * 256)
        total = TT[4, rows, :]
        OB[s] = (ACC[4, rows, :] / total).astype(bf16)
        both = jnp.where(lane == 0, PK[4, rows, :], total)
        ST[s] = jnp.transpose(both)[:8, :]

    def back_copy(d, kind):
        s = plane_peer(d)
        src, dst = ((OB, RO), (ST, RST))[kind]
        return pltpu.make_async_remote_copy(
            src.at[s], dst.at[i], r_ss.at[d - 1, kind], r_rs.at[d - 1, kind],
            device_id=dev(z, s), device_id_type=MESH)

    def back_arrived(d, kind):
        s = (i + 4 - d) % 4
        src, dst = ((OB, RO), (ST, RST))[kind]
        return pltpu.make_async_remote_copy(
            src.at[i], dst.at[s], r_ss.at[d - 1, kind], r_rs.at[d - 1, kind],
            device_id=dev(z, s), device_id_type=MESH)

    for d in (2, 3, 1):
        for kind in range(2):
            back_copy(d, kind).start()
    RO[i] = OB[i]
    RST[i] = ST[i]

    for d in (1, 3, 2):
        for yr in range(2):
            w_arrived(d, yr).wait_recv()
            w_forward(d, yr).start()

    for d in (1, 2, 3):
        for kind in range(2):
            back_arrived(d, kind).wait_recv()
    for s in range(HEADS):
        stats = jnp.transpose(RST[s])
        peak = jnp.broadcast_to(stats[:, 0:1], (256, DH))
        total = jnp.broadcast_to(stats[:, 1:2], (256, DH))
        picked = (s, pl.ds(s, 256, stride=4), slice(None))
        near = (ACC[picked], PK[picked], TT[picked])
        numer, _, whole = merge(near, (RO[s].astype(f32) * total, peak, total))
        ACC[picked] = numer
        TT[picked] = whole
        att_ref[:, s * DH:(s + 1) * DH] = (ACC[s] / TT[s]).astype(bf16)

    for d in (1, 2, 3):
        for yr in range(2):
            w_copy(d, yr).wait_send()
            w_forward(d, yr).wait_send()
            w_forwarded(d, yr).wait_recv()
        for kind in range(4):
            plane_copy(d, kind).wait_send()
        for kind in range(2):
            back_copy(d, kind).wait_send()
    for yr in range(2):
        w_own(yr).wait()
    for hop in range(nfwd):
        forward(hop, (z + planes - hop) % planes).wait_send()
    for hop in range(nbwd):
        backward(hop, (z + hop) % planes).wait_send()

    @pl.when(zpar == 0)
    def _():
        for s in range(4):
            prev_copy(s).wait_send()

    @pl.when(core == 0)
    def _():
        for h in range(HEADS):
            for a in range(2):
                near_copy(h, a).wait_send()


def project_kernel(
    att_ref, wg_ref, out_ref, AL, AR, AO, PS, PR, OWN, OTH,
    r_ss, r_rs, l_ss, l_rs, or_ss, or_rs, ol_ss, ol_rs, y_ss, y_rs,
):
    seq = lax.axis_index("seq")
    head = lax.axis_index("head")
    x = head % 4
    y = head // 4
    right = (seq, y * 4 + (x + 1) % 4)
    left = (seq, y * 4 + (x + 3) % 4)
    across = (seq, (1 - y) * 4 + x)
    steps = ROWS // TILE
    halfrows = TILE // 2

    barrier = pltpu.get_barrier_semaphore()
    for target in (right, left, across):
        pl.semaphore_signal(barrier, inc=1, device_id=target, device_id_type=MESH)
    pl.semaphore_wait(barrier, 3)

    def rows_of(t):
        return pl.ds(pl.multiple_of(t * TILE, TILE), TILE)

    def to_right(t):
        return pltpu.make_async_remote_copy(
            att_ref.at[rows_of(t)], AL.at[rows_of(t)], r_ss.at[t], r_rs.at[t], device_id=right, device_id_type=MESH)

    def to_left(t):
        return pltpu.make_async_remote_copy(
            att_ref.at[rows_of(t)], AR.at[rows_of(t)], l_ss.at[t], l_rs.at[t], device_id=left, device_id_type=MESH)

    def relay_right(t):
        part = pl.ds(pl.multiple_of(t * TILE, halfrows), halfrows)
        return pltpu.make_async_remote_copy(
            AL.at[part], AO.at[part], or_ss.at[t], or_rs.at[t], device_id=right, device_id_type=MESH)

    def relay_left(t):
        part = pl.ds(pl.multiple_of(t * TILE + halfrows, halfrows), halfrows)
        return pltpu.make_async_remote_copy(
            AR.at[part], AO.at[part], ol_ss.at[t], ol_rs.at[t], device_id=left, device_id_type=MESH)

    def to_across(t):
        return pltpu.make_async_remote_copy(
            PS.at[rows_of(t)], PR.at[rows_of(t)], y_ss.at[t], y_rs.at[t], device_id=across, device_id_type=MESH)

    def start_tile(t):
        to_right(t).start()
        to_left(t).start()

    def mm(a, yr, xi):
        return jnp.dot(a, wg_ref[yr, xi], preferred_element_type=f32)

    def finish(t):
        relay_right(t).wait_recv()
        relay_left(t).wait_recv()
        far = AO[rows_of(t), :]
        PS[rows_of(t), :] = (OTH[rows_of(t), :] + mm(far, 1, (x + 2) % 4)).astype(bf16)
        to_across(t).start()
        OWN[rows_of(t), :] = OWN[rows_of(t), :] + mm(far, 0, (x + 2) % 4)

    start_tile(0)
    start_tile(1)

    def step(t, carry):
        to_right(t).wait_recv()
        relay_right(t).start()
        to_left(t).wait_recv()
        relay_left(t).start()

        @pl.when(t + 2 < steps)
        def _():
            start_tile(t + 2)

        here, from_left, from_right = att_ref[rows_of(t), :], AL[rows_of(t), :], AR[rows_of(t), :]
        for yr, acc in ((1, OTH), (0, OWN)):
            acc[rows_of(t), :] = (
                mm(here, yr, x) + mm(from_left, yr, (x + 3) % 4) + mm(from_right, yr, (x + 1) % 4))

        @pl.when(t >= 1)
        def _():
            finish(t - 1)

        return carry

    lax.fori_loop(0, steps, step, 0)
    finish(steps - 1)

    def close(t, carry):
        to_across(t).wait_recv()
        out_ref[rows_of(t), :] = (OWN[rows_of(t), :] + PR[rows_of(t), :].astype(f32)).astype(bf16)
        to_right(t).wait_send()
        to_left(t).wait_send()
        relay_right(t).wait_send()
        relay_left(t).wait_send()
        to_across(t).wait_send()
        return carry

    lax.fori_loop(0, steps, close, 0)


def shards(planes, queries, keys, values, out_weight):
    dma = pltpu.SemaphoreType.DMA
    vmem = pltpu.VMEM
    anywhere = pl.BlockSpec(memory_space=pl.ANY)
    inside = pl.BlockSpec(memory_space=pltpu.VMEM)
    attended, weight = pl.pallas_call(
        functools.partial(attend_kernel, planes),
        name="attend",
        out_shape=(
            jax.ShapeDtypeStruct((ROWS, HEADS * DH), bf16),
            jax.ShapeDtypeStruct((2, 4, 512, 512), bf16),
        ),
        in_specs=[anywhere] * 4,
        out_specs=(inside, anywhere),
        scratch_shapes=[
            vmem((5, ROWS, DH), bf16),
            vmem((5, 2, 2 * ROWS, DH), bf16),
            vmem((4, 3, 256, DH), bf16),
            vmem((4, 3, 64, DH), bf16),
            vmem((256, DH), bf16),
            vmem((planes, 2, 256, DH), bf16),
            vmem((5, ROWS, DH), f32),
            vmem((5, ROWS, DH), f32),
            vmem((5, ROWS, DH), f32),
            vmem((3, ROWS, DH), f32),
            vmem((4, 256, DH), bf16),
            vmem((4, 8, 256), f32),
            vmem((4, 256, DH), bf16),
            vmem((4, 8, 256), f32),
            dma((4, 3)), dma((2,)),
            dma((3, 2)), dma((3, 2)), dma((3, 2)), dma((3, 2)),
            dma((4, 2)), dma((4, 2)),
            dma((3, 4)), dma((3, 4)),
            dma((4,)), dma((4,)),
            dma((4,)), dma((4,)), dma((4,)), dma((4,)),
            dma((3, 2)), dma((3, 2)),
        ],
        compiler_params=pltpu.CompilerParams(
            collective_id=0, has_side_effects=True, vmem_limit_bytes=56 * 1024 * 1024),
    )(queries, keys, values, out_weight)
    return pl.pallas_call(
        project_kernel,
        name="project",
        out_shape=jax.ShapeDtypeStruct((ROWS, 512), bf16),
        in_specs=[inside, inside],
        out_specs=inside,
        scratch_shapes=[vmem((ROWS, 512), bf16)] * 5 + [vmem((ROWS, 512), f32)] * 2 + [dma((4,))] * 10,
        compiler_params=pltpu.CompilerParams(
            collective_id=1, has_side_effects=True, vmem_limit_bytes=48 * 1024 * 1024),
    )(attended, weight)


def solution(mesh):
    placed = (P("seq", "head"), P("seq", "head"), P("seq", "head"), P("head", None))
    planes = mesh.shape["seq"] // 4
    return jax.shard_map(
        functools.partial(shards, planes), mesh=mesh, in_specs=placed, out_specs=P("seq", "head"), check_vma=False
    )
```

```python
import functools
import math

import jax
import jax.numpy as jnp
from jax import lax
from jax.experimental import pallas as pl
from jax.experimental.pallas import tpu as pltpu
from jax.sharding import PartitionSpec as P

DH = 128
ROWS = 1024
HEADS = 4
TILE = 256
NEG = -1e30
SCALE2 = math.log2(math.e) / math.sqrt(DH)
MESH = pl.DeviceIdType.MESH
bf16 = jnp.bfloat16
f32 = jnp.float32


def nt_dot(a, b):
    return lax.dot_general(a, b, (((1,), (1,)), ((), ())), preferred_element_type=f32)


def softmax_pieces(query, pieces):
    scores = []
    for key_rows, _, limit in pieces:
        score = nt_dot(query, key_rows)
        if limit is not None:
            row = lax.broadcasted_iota(jnp.int32, score.shape, 0)
            col = lax.broadcasted_iota(jnp.int32, score.shape, 1)
            score = jnp.where(col - row <= limit, score, NEG)
        scores.append(score)
    peak = functools.reduce(jnp.maximum, [jnp.max(s, axis=1, keepdims=True) for s in scores])
    both = None
    for score, (_, value_rows, _) in zip(scores, pieces):
        weights = jnp.exp2((score - peak) * SCALE2).astype(bf16)
        ones = jnp.ones(value_rows.shape, bf16)
        term = jnp.dot(weights, jnp.concatenate([value_rows, ones], axis=1), preferred_element_type=f32)
        both = term if both is None else both + term
    numer, total = both[:, :DH], both[:, DH:]
    return numer, jnp.broadcast_to(peak, numer.shape), total


def merge(one, two):
    numer1, peak1, total1 = one
    numer2, peak2, total2 = two
    top = jnp.maximum(peak1, peak2)
    f1 = jnp.exp2((peak1 - top) * SCALE2)
    f2 = jnp.exp2((peak2 - top) * SCALE2)
    return numer1 * f1 + numer2 * f2, top, total1 * f1 + total2 * f2


def layer_kernel(
    planes,
    q_hbm, k_hbm, v_hbm, w_hbm, out_ref,
    QA, KV, SM, SF, FQ, FKV, ACC, PK, TT, TMP, RO, RST, OB, ST, CQ, WG, AG, PS, PR, OWN, OTH,
    loc, locw, w_ss, w_rs, wf_ss, wf_rs, n_ss, n_rs, p_ss, p_rs, cq_ss, cq_rs,
    f_ss, f_rs, b_ss, b_rs, r_ss, r_rs, cr_ss, cr_rs,
    ar_ss, ar_rs, al_ss, al_rs, or_ss, or_rs, ol_ss, ol_rs, y_ss, y_rs,
):
    seq = lax.axis_index("seq")
    head = lax.axis_index("head")
    z = seq // 4
    i = seq % 4
    core = seq % 2
    zpar = z % 2
    x = head % 4
    y = head // 4

    def dev(plane, slot):
        return (plane * 4 + slot, head)

    def plane_peer(d):
        return (i + d) % 4

    pair = z + 1 - 2 * zpar
    znext = (z + 1) % planes
    zprev = (z + planes - 1) % planes
    zother = (z + planes - 1 + 2 * zpar) % planes

    loads = []
    for h in range(HEADS):
        cols = slice(h * DH, (h + 1) * DH)
        loads.append([
            pltpu.make_async_copy(q_hbm.at[:, cols], QA.at[h], loc.at[h, 0]),
            pltpu.make_async_copy(k_hbm.at[:, cols], KV.at[h, 0, pl.ds(ROWS, ROWS)], loc.at[h, 1]),
            pltpu.make_async_copy(v_hbm.at[:, cols], KV.at[h, 1, pl.ds(ROWS, ROWS)], loc.at[h, 2]),
        ])
        for copy in loads[-1]:
            copy.start()

    def w_own(yr):
        col = pl.multiple_of((((y + yr) % 2) * 4 + x) * 512, 512)
        return pltpu.make_async_copy(w_hbm.at[:, pl.ds(col, 512)], WG.at[yr, x], locw.at[yr])

    for yr in range(2):
        w_own(yr).start()

    barrier = pltpu.get_barrier_semaphore()
    greet = [dev(z, plane_peer(d)) for d in (1, 2, 3)]
    greet += [dev(pair, s) for s in range(4)]
    greet += [dev(zother, i)]
    greet += [(seq, y * 4 + (x + d) % 4) for d in (1, 2, 3)]
    right = (seq, y * 4 + (x + 1) % 4)
    left = (seq, y * 4 + (x + 3) % 4)
    across = (seq, (1 - y) * 4 + x)
    greet += [across]
    for target in greet:
        pl.semaphore_signal(barrier, inc=1, device_id=target, device_id_type=MESH)
    pl.semaphore_wait(barrier, len(greet))

    def near_copy(h, a):
        src = (k_hbm, v_hbm)[a].at[:, h * DH:(h + 1) * DH]
        return pltpu.make_async_remote_copy(
            src, KV.at[h, a, pl.ds(0, ROWS)], n_ss.at[h, a], n_rs.at[h, a],
            device_id=dev(z, i + 1 - 2 * core), device_id_type=MESH)

    @pl.when(core == 0)
    def _():
        for h in range(HEADS):
            for a in range(2):
                near_copy(h, a).start()

    half = pl.multiple_of(core * 256, 256)

    def w_copy(d, yr):
        xd = (x + d) % 4
        yd = (y + yr) % 2
        col = pl.multiple_of((yd * 4 + xd) * 512, 512)
        return pltpu.make_async_remote_copy(
            w_hbm.at[pl.ds(half, 256), pl.ds(col, 512)],
            WG.at[yr, x, pl.ds(half, 256)],
            w_ss.at[d - 1, yr], w_rs.at[d - 1, yr],
            device_id=(seq, y * 4 + xd), device_id_type=MESH)

    def w_arrived(d, yr):
        xs = (x + 4 - d) % 4
        return pltpu.make_async_remote_copy(
            WG.at[yr, xs, pl.ds(half, 256)],
            WG.at[yr, xs, pl.ds(half, 256)],
            w_ss.at[d - 1, yr], w_rs.at[d - 1, yr],
            device_id=(seq, y * 4 + xs), device_id_type=MESH)

    def w_forward(d, yr):
        xs = (x + 4 - d) % 4
        return pltpu.make_async_remote_copy(
            WG.at[yr, xs, pl.ds(half, 256)],
            WG.at[yr, xs, pl.ds(half, 256)],
            wf_ss.at[d - 1, yr], wf_rs.at[d - 1, yr],
            device_id=dev(z, i + 1 - 2 * core), device_id_type=MESH)

    def w_forwarded(d, yr):
        xs = (x + 4 - d) % 4
        other = pl.multiple_of(256 - half, 256)
        return pltpu.make_async_remote_copy(
            WG.at[yr, xs, pl.ds(other, 256)],
            WG.at[yr, xs, pl.ds(other, 256)],
            wf_ss.at[d - 1, yr], wf_rs.at[d - 1, yr],
            device_id=dev(z, i + 1 - 2 * core), device_id_type=MESH)

    for d in (1, 3, 2):
        for yr in range(2):
            w_copy(d, yr).start()

    for h in range(HEADS):
        for a in range(3):
            loads[h][a].wait()
            source = QA[h] if a == 0 else KV[h, a - 1, ROWS:, :]
            TMP[a] = source.astype(f32)
            SM[h, a] = TMP[a, pl.ds(h, 256, stride=4), :].astype(bf16)
            SF[h, a] = TMP[a, pl.ds(4 * x + h, 64, stride=16), :].astype(bf16)

    def plane_copy(d, kind):
        s = plane_peer(d)
        return plane_descriptor(d, kind, s, i, s)

    def plane_arrived(d, kind):
        s = (i + 4 - d) % 4
        return plane_descriptor(d, kind, s, s, i)

    def plane_descriptor(d, kind, target, sender, slot):
        mid = pl.multiple_of(sender * 256, 256)
        far = pl.multiple_of(sender * 64, 64)
        src, dst = (
            (SF.at[slot, pl.ds(1, 2)], FKV.at[z, :, pl.ds(far, 64)]),
            (SF.at[slot, 0], FQ.at[pl.ds(far, 64)]),
            (SM.at[slot, pl.ds(1, 2)], KV.at[4, :, pl.ds(ROWS + mid, 256)]),
            (SM.at[slot, 0], QA.at[4, pl.ds(mid, 256)]),
        )[kind]
        return pltpu.make_async_remote_copy(
            src, dst, p_ss.at[d - 1, kind], p_rs.at[d - 1, kind],
            device_id=dev(z, target), device_id_type=MESH)

    def cross_query(s, sender):
        return pltpu.make_async_remote_copy(
            SM.at[s, 0], CQ.at[pl.ds(pl.multiple_of(sender * 256, 256), 256)],
            cq_ss.at[s], cq_rs.at[sender], device_id=dev(pair, s), device_id_type=MESH)

    for kind in (0, 1):
        for d in (2, 3, 1):
            plane_copy(d, kind).start()

    for kind in (2, 3):
        for d in (2, 3, 1):
            plane_copy(d, kind).start()

    @pl.when(zpar == 1)
    def _():
        for s in range(4):
            cross_query(s, i).start()

    own_mid = pl.multiple_of(i * 256, 256)
    own_far = pl.multiple_of(i * 64, 64)
    QA[4, pl.ds(own_mid, 256), :] = SM[i, 0]
    FQ[pl.ds(own_far, 64), :] = SF[i, 0]
    for a in range(2):
        KV[4, a, pl.ds(ROWS + own_mid, 256), :] = SM[i, 1 + a]
        FKV[z, a, pl.ds(own_far, 64), :] = SF[i, 1 + a]

    def forward(hop, slot):
        return pltpu.make_async_remote_copy(
            FKV.at[slot], FKV.at[slot], f_ss.at[hop], f_rs.at[hop],
            device_id=dev(znext, i), device_id_type=MESH)

    def backward(hop, slot):
        return pltpu.make_async_remote_copy(
            FKV.at[slot], FKV.at[slot], b_ss.at[hop], b_rs.at[hop],
            device_id=dev(zprev, i), device_id_type=MESH)

    def tiles(h, with_prev):
        for b in range(ROWS // TILE):
            rows = slice(b * TILE, (b + 1) * TILE)
            pieces = []
            if with_prev:
                pieces.append((KV[h, 0, :ROWS, :], KV[h, 1, :ROWS, :], None))
            if b:
                pieces.append((KV[h, 0, ROWS:ROWS + b * TILE, :], KV[h, 1, ROWS:ROWS + b * TILE, :], None))
            diag = slice(ROWS + b * TILE, ROWS + (b + 1) * TILE)
            pieces.append((KV[h, 0, diag, :], KV[h, 1, diag, :], 0))
            numer, peak, total = softmax_pieces(QA[h, rows, :], pieces)
            ACC[h, rows, :] = numer
            PK[h, rows, :] = peak
            TT[h, rows, :] = total

    def x_copy(part, sem):
        return (
            pltpu.make_async_remote_copy(
                AG.at[(0,) + part], AG.at[(1,) + part], ar_ss.at[sem], ar_rs.at[sem],
                device_id=right, device_id_type=MESH),
            pltpu.make_async_remote_copy(
                AG.at[(0,) + part], AG.at[(3,) + part], al_ss.at[sem], al_rs.at[sem],
                device_id=left, device_id_type=MESH),
        )

    def x_relay(part, sem):
        top = part + (pl.ds(0, 128),)
        low = part + (pl.ds(128, 128),)
        return (
            pltpu.make_async_remote_copy(
                AG.at[(1,) + top], AG.at[(2,) + top], or_ss.at[sem], or_rs.at[sem],
                device_id=right, device_id_type=MESH),
            pltpu.make_async_remote_copy(
                AG.at[(3,) + low], AG.at[(2,) + low], ol_ss.at[sem], ol_rs.at[sem],
                device_id=left, device_id_type=MESH),
        )

    def x_pass_on(part, sem):
        for arrived, onward in zip(x_copy(part, sem), x_relay(part, sem)):
            arrived.wait_recv()
            onward.start()

    def near_part(h):
        return (h, pl.ds(1, 3))

    def strided_part(h):
        return (h, 0)

    nfwd = planes // 2
    nbwd = planes - 1 - nfwd

    def level_step(h, carry):
        @pl.when((h < 4) & (core == 1))
        def _():
            for a in range(2):
                pltpu.make_async_remote_copy(
                    KV.at[h, a, pl.ds(0, ROWS)], KV.at[h, a, pl.ds(0, ROWS)], n_ss.at[h, a], n_rs.at[h, a],
                    device_id=dev(z, i + 1 - 2 * core), device_id_type=MESH).wait_recv()

        @pl.when(h == 4)
        def _():
            for kind in (2, 3):
                for d in (1, 2, 3):
                    plane_arrived(d, kind).wait_recv()

        parity = jnp.where(h < 4, core, 0)

        @pl.when(parity == 1)
        def _():
            tiles(h, True)

        @pl.when(parity == 0)
        def _():
            tiles(h, False)

        @pl.when(h == 0)
        def _():
            for kind in (0, 1):
                for d in (1, 2, 3):
                    plane_arrived(d, kind).wait_recv()

        @pl.when((h >= 1) & (h <= nfwd))
        def _():
            forward(h - 1, (z + planes - h) % planes).wait_recv()

        @pl.when((h >= 1) & (h <= nbwd))
        def _():
            backward(h - 1, (z + h) % planes).wait_recv()

        @pl.when(h < nfwd)
        def _():
            forward(h, (z + planes - h) % planes).start()

        @pl.when(h < nbwd)
        def _():
            backward(h, (z + h) % planes).start()

        @pl.when(h < 4)
        def _():
            for rr in range(1, 4):
                picked = (h, pl.ds((h + rr) % 4, 256, stride=4), slice(None))
                AG[0, h, rr] = (ACC[picked] / TT[picked]).astype(bf16)
            for copy in x_copy(near_part(h), h):
                copy.start()

        return carry

    lax.fori_loop(0, HEADS + 1, level_step, 0)

    lane = lax.broadcasted_iota(jnp.int32, (256, DH), 1)

    def pack(slot, numer, peak, total):
        OB[slot] = (numer / total).astype(bf16)
        ST[slot] = jnp.transpose(jnp.where(lane == 0, peak, total))[:8, :]

    def cross_result(s, sender, kind):
        src, dst = ((OB, RO), (ST, RST))[kind]
        return pltpu.make_async_remote_copy(
            src.at[4 + s], dst.at[4 + sender], cr_ss.at[s, kind], cr_rs.at[sender, kind],
            device_id=dev(pair, s), device_id_type=MESH)

    @pl.when(zpar == 0)
    def _():
        for s in range(4):
            cross_query(s, s).wait_recv()
            rows = slice(s * 256, (s + 1) * 256)
            pack(4 + s, *softmax_pieces(CQ[rows, :], [(KV[4, 0, ROWS:, :], KV[4, 1, ROWS:, :], None)]))
            for kind in range(2):
                cross_result(s, i, kind).start()

    far_pieces = [(FKV[j, 0], FKV[j, 1], TILE * (z - j)) for j in range(planes)]
    far = softmax_pieces(FQ[...], far_pieces)
    picked = (4, pl.ds(x, 256, stride=4), slice(None))
    mid = (ACC[picked], PK[picked], TT[picked])
    ACC[picked], PK[picked], TT[picked] = merge(mid, far)
    for s in range(4):
        rows = slice(s * 256, (s + 1) * 256)
        pack(s, ACC[4, rows, :], PK[4, rows, :], TT[4, rows, :])

    def back_copy(d, kind):
        s = plane_peer(d)
        src, dst = ((OB, RO), (ST, RST))[kind]
        return pltpu.make_async_remote_copy(
            src.at[s], dst.at[i], r_ss.at[d - 1, kind], r_rs.at[d - 1, kind],
            device_id=dev(z, s), device_id_type=MESH)

    def back_arrived(d, kind):
        s = (i + 4 - d) % 4
        src, dst = ((OB, RO), (ST, RST))[kind]
        return pltpu.make_async_remote_copy(
            src.at[i], dst.at[s], r_ss.at[d - 1, kind], r_rs.at[d - 1, kind],
            device_id=dev(z, s), device_id_type=MESH)

    for d in (2, 3, 1):
        for kind in range(2):
            back_copy(d, kind).start()
    RO[i] = OB[i]
    RST[i] = ST[i]

    for d in (1, 3, 2):
        for yr in range(2):
            w_arrived(d, yr).wait_recv()
            w_forward(d, yr).start()

    for d in (1, 2, 3):
        for kind in range(2):
            back_arrived(d, kind).wait_recv()

    @pl.when(zpar == 1)
    def _():
        for s in range(4):
            for kind in range(2):
                cross_result(s, s, kind).wait_recv()

    def unpack(slot):
        stats = jnp.transpose(RST[slot])
        peak = jnp.broadcast_to(stats[:, 0:1], (256, DH))
        total = jnp.broadcast_to(stats[:, 1:2], (256, DH))
        return RO[slot].astype(f32) * total, peak, total

    for s in range(HEADS):
        picked = (s, pl.ds(s, 256, stride=4), slice(None))
        state = merge((ACC[picked], PK[picked], TT[picked]), unpack(s))

        @pl.when(zpar == 0)
        def _():
            AG[0, s, 0] = (state[0] / state[2]).astype(bf16)

        @pl.when(zpar == 1)
        def _():
            numer, _, total = merge(state, unpack(4 + s))
            AG[0, s, 0] = (numer / total).astype(bf16)

        for copy in x_copy(strided_part(s), 4 + s):
            copy.start()

    for h in range(HEADS):
        x_pass_on(near_part(h), h)
    for d in (1, 2, 3):
        for yr in range(2):
            w_forwarded(d, yr).wait_recv()
    for yr in range(2):
        w_own(yr).wait()

    def weight(yr, j, h):
        return WG[yr, (x + 4 - j) % 4, h * DH:(h + 1) * DH, :]

    def product(r, yr, blocks):
        left_side = jnp.concatenate([AG[j, h, (r - h) % 4] for j, h in blocks], axis=1)
        right_side = jnp.concatenate([weight(yr, j, h) for j, h in blocks], axis=0)
        return jnp.dot(left_side, right_side, preferred_element_type=f32)

    for r in range(4):
        blocks = [(j, h) for j in (0, 1, 3) for h in range(HEADS) if h != r]
        for yr, acc in ((1, OTH), (0, OWN)):
            acc[r] = product(r, yr, blocks)

    def to_across(r):
        return pltpu.make_async_remote_copy(
            PS.at[r], PR.at[r], y_ss.at[r], y_rs.at[r], device_id=across, device_id_type=MESH)

    for h in range(HEADS):
        x_pass_on(strided_part(h), 4 + h)
    for h in range(HEADS):
        for copy in x_relay(near_part(h), h):
            copy.wait_recv()
    for r in range(4):
        for copy in x_relay(strided_part(r), 4 + r):
            copy.wait_recv()
        blocks = [(2, h) for h in range(HEADS) if h != r] + [(j, r) for j in range(4)]
        PS[r] = (OTH[r] + product(r, 1, blocks)).astype(bf16)
        to_across(r).start()
        OWN[r] = OWN[r] + product(r, 0, blocks)

    for r in range(4):
        to_across(r).wait_recv()
        mixed = OWN[r] + PR[r].astype(f32)
        for c in range(4):
            ACC[c, pl.ds(r, 256, stride=4), :] = mixed[:, c * DH:(c + 1) * DH]
    for c in range(4):
        out_ref[:, c * DH:(c + 1) * DH] = ACC[c].astype(bf16)

    for d in (1, 2, 3):
        for yr in range(2):
            w_copy(d, yr).wait_send()
            w_forward(d, yr).wait_send()
        for kind in range(4):
            plane_copy(d, kind).wait_send()
        for kind in range(2):
            back_copy(d, kind).wait_send()
    for hop in range(nfwd):
        forward(hop, (z + planes - hop) % planes).wait_send()
    for hop in range(nbwd):
        backward(hop, (z + hop) % planes).wait_send()
    for h in range(HEADS):
        for part, sem in ((near_part(h), h), (strided_part(h), 4 + h)):
            for copy in x_copy(part, sem) + x_relay(part, sem):
                copy.wait_send()
        to_across(h).wait_send()

    @pl.when(zpar == 1)
    def _():
        for s in range(4):
            cross_query(s, i).wait_send()

    @pl.when(zpar == 0)
    def _():
        for s in range(4):
            for kind in range(2):
                cross_result(s, i, kind).wait_send()

    @pl.when(core == 0)
    def _():
        for h in range(HEADS):
            for a in range(2):
                near_copy(h, a).wait_send()


def shards(planes, queries, keys, values, out_weight):
    dma = pltpu.SemaphoreType.DMA
    vmem = pltpu.VMEM
    anywhere = pl.BlockSpec(memory_space=pl.ANY)
    return pl.pallas_call(
        functools.partial(layer_kernel, planes),
        name="layer",
        out_shape=jax.ShapeDtypeStruct((ROWS, HEADS * DH), bf16),
        in_specs=[anywhere] * 4,
        out_specs=pl.BlockSpec(memory_space=pltpu.VMEM),
        scratch_shapes=[
            vmem((5, ROWS, DH), bf16),
            vmem((5, 2, 2 * ROWS, DH), bf16),
            vmem((4, 3, 256, DH), bf16),
            vmem((4, 3, 64, DH), bf16),
            vmem((256, DH), bf16),
            vmem((planes, 2, 256, DH), bf16),
            vmem((5, ROWS, DH), f32),
            vmem((5, ROWS, DH), f32),
            vmem((5, ROWS, DH), f32),
            vmem((3, ROWS, DH), f32),
            vmem((8, 256, DH), bf16),
            vmem((8, 8, 256), f32),
            vmem((8, 256, DH), bf16),
            vmem((8, 8, 256), f32),
            vmem((ROWS, DH), bf16),
            vmem((2, 4, 512, 512), bf16),
            vmem((4, 4, 4, 256, DH), bf16),
            vmem((4, 256, 512), bf16),
            vmem((4, 256, 512), bf16),
            vmem((4, 256, 512), f32),
            vmem((4, 256, 512), f32),
            dma((4, 3)), dma((2,)),
            dma((3, 2)), dma((3, 2)), dma((3, 2)), dma((3, 2)),
            dma((4, 2)), dma((4, 2)),
            dma((3, 4)), dma((3, 4)),
            dma((4,)), dma((4,)),
            dma((4,)), dma((4,)), dma((4,)), dma((4,)),
            dma((3, 2)), dma((3, 2)),
            dma((4, 2)), dma((4, 2)),
        ] + [dma((8,))] * 8 + [dma((4,))] * 2,
        compiler_params=pltpu.CompilerParams(
            collective_id=0, has_side_effects=True, vmem_limit_bytes=58 * 1024 * 1024),
    )(queries, keys, values, out_weight)


def solution(mesh):
    placed = (P("seq", "head"), P("seq", "head"), P("seq", "head"), P("head", None))
    planes = mesh.shape["seq"] // 4
    return jax.shard_map(
        functools.partial(shards, planes), mesh=mesh, in_specs=placed, out_specs=P("seq", "head"), check_vma=False
    )
```

```python
import functools
import math

import jax
import jax.numpy as jnp
from jax import lax
from jax.experimental import pallas as pl
from jax.experimental.pallas import tpu as pltpu
from jax.sharding import PartitionSpec as P

DH = 128
ROWS = 1024
HEADS = 4
TILE = 256
NEG = -1e30
SCALE2 = math.log2(math.e) / math.sqrt(DH)
MESH = pl.DeviceIdType.MESH
bf16 = jnp.bfloat16
f32 = jnp.float32


def nt_dot(a, b):
    return lax.dot_general(a, b, (((1,), (1,)), ((), ())), preferred_element_type=f32)


def softmax_pieces(query, pieces):
    scores = []
    for key_rows, _, limit in pieces:
        score = nt_dot(query, key_rows)
        if limit is not None:
            row = lax.broadcasted_iota(jnp.int32, score.shape, 0)
            col = lax.broadcasted_iota(jnp.int32, score.shape, 1)
            score = jnp.where(col - row <= limit, score, NEG)
        scores.append(score)
    peak = functools.reduce(jnp.maximum, [jnp.max(s, axis=1, keepdims=True) for s in scores])
    both = None
    for score, (_, value_rows, _) in zip(scores, pieces):
        weights = jnp.exp2((score - peak) * SCALE2).astype(bf16)
        ones = jnp.ones(value_rows.shape, bf16)
        term = jnp.dot(weights, jnp.concatenate([value_rows, ones], axis=1), preferred_element_type=f32)
        both = term if both is None else both + term
    numer, total = both[:, :DH], both[:, DH:]
    return numer, jnp.broadcast_to(peak, numer.shape), total


def merge(one, two):
    numer1, peak1, total1 = one
    numer2, peak2, total2 = two
    top = jnp.maximum(peak1, peak2)
    f1 = jnp.exp2((peak1 - top) * SCALE2)
    f2 = jnp.exp2((peak2 - top) * SCALE2)
    return numer1 * f1 + numer2 * f2, top, total1 * f1 + total2 * f2


def layer_kernel(
    planes,
    q_hbm, k_hbm, v_hbm, w_hbm, out_ref,
    QA, KV, SM, SF, FQ, FKV, ACC, PK, TT, TMP, RO, RST, OB, ST, CQ, WG, AG, PS, PR, OWN, OTH,
    loc, locw, w_ss, w_rs, wy_ss, wy_rs, wf_ss, wf_rs, wg_ss, wg_rs, n_ss, n_rs, p_ss, p_rs, cq_ss, cq_rs,
    f_ss, f_rs, b_ss, b_rs, r_ss, r_rs, cr_ss, cr_rs,
    ar_ss, ar_rs, al_ss, al_rs, or_ss, or_rs, ol_ss, ol_rs, y_ss, y_rs,
):
    seq = lax.axis_index("seq")
    head = lax.axis_index("head")
    z = seq // 4
    i = seq % 4
    core = seq % 2
    zpar = z % 2
    x = head % 4
    y = head // 4

    def dev(plane, slot):
        return (plane * 4 + slot, head)

    def plane_peer(d):
        return (i + d) % 4

    pair = z + 1 - 2 * zpar
    znext = (z + 1) % planes
    zprev = (z + planes - 1) % planes
    zother = (z + planes - 1 + 2 * zpar) % planes

    loads = []
    for h in range(HEADS):
        cols = slice(h * DH, (h + 1) * DH)
        loads.append([
            pltpu.make_async_copy(q_hbm.at[:, cols], QA.at[h], loc.at[h, 0]),
            pltpu.make_async_copy(k_hbm.at[:, cols], KV.at[h, 0, pl.ds(ROWS, ROWS)], loc.at[h, 1]),
            pltpu.make_async_copy(v_hbm.at[:, cols], KV.at[h, 1, pl.ds(ROWS, ROWS)], loc.at[h, 2]),
        ])
        for copy in loads[-1]:
            copy.start()

    def w_own(yr):
        col = pl.multiple_of((((y + yr) % 2) * 4 + x) * 512, 512)
        return pltpu.make_async_copy(w_hbm.at[:, pl.ds(col, 512)], WG.at[yr, x], locw.at[yr])

    for yr in range(2):
        w_own(yr).start()

    barrier = pltpu.get_barrier_semaphore()
    greet = [dev(z, plane_peer(d)) for d in (1, 2, 3)]
    greet += [dev(pair, s) for s in range(4)]
    greet += [dev(zother, i)]
    greet += [(seq, y * 4 + (x + d) % 4) for d in (1, 2, 3)]
    right = (seq, y * 4 + (x + 1) % 4)
    left = (seq, y * 4 + (x + 3) % 4)
    across = (seq, (1 - y) * 4 + x)
    greet += [across]
    for target in greet:
        pl.semaphore_signal(barrier, inc=1, device_id=target, device_id_type=MESH)
    pl.semaphore_wait(barrier, len(greet))

    def near_copy(h, a):
        src = (k_hbm, v_hbm)[a].at[:, h * DH:(h + 1) * DH]
        return pltpu.make_async_remote_copy(
            src, KV.at[h, a, pl.ds(0, ROWS)], n_ss.at[h, a], n_rs.at[h, a],
            device_id=dev(z, i + 1 - 2 * core), device_id_type=MESH)

    @pl.when(core == 0)
    def _():
        for h in range(HEADS):
            for a in range(2):
                near_copy(h, a).start()

    chip_mate = i + 1 - 2 * core
    y_mate = (i + 2) % 4

    def quarter(slot):
        return pl.ds(pl.multiple_of(slot * 128, 128), 128)

    def w_copy(d, yr):
        xd = (x + d) % 4
        yd = (y + yr) % 2
        col = pl.multiple_of((yd * 4 + xd) * 512, 512)
        return pltpu.make_async_remote_copy(
            w_hbm.at[quarter(i), pl.ds(col, 512)], WG.at[yr, x, quarter(i)],
            w_ss.at[d - 1, yr], w_rs.at[d - 1, yr],
            device_id=(seq, y * 4 + xd), device_id_type=MESH)

    def w_share(d, yr, slot, sems, target):
        piece = WG.at[yr, (x + 4 - d) % 4, quarter(slot)]
        return pltpu.make_async_remote_copy(
            piece, piece, sems[0].at[d - 1, yr], sems[1].at[d - 1, yr],
            device_id=target, device_id_type=MESH)

    def w_arrived(d, yr):
        return w_share(d, yr, i, (w_ss, w_rs), (seq, y * 4 + (x + 4 - d) % 4))

    def w_cross(d, yr):
        return w_share(d, yr, i, (wy_ss, wy_rs), dev(z, y_mate))

    def w_crossed(d, yr):
        return w_share(d, yr, y_mate, (wy_ss, wy_rs), dev(z, y_mate))

    def w_chip(d, yr):
        return w_share(d, yr, i, (wf_ss, wf_rs), dev(z, chip_mate))

    def w_chipped(d, yr):
        return w_share(d, yr, chip_mate, (wf_ss, wf_rs), dev(z, chip_mate))

    def w_last(d, yr):
        return w_share(d, yr, y_mate, (wg_ss, wg_rs), dev(z, chip_mate))

    def w_lasted(d, yr):
        return w_share(d, yr, (chip_mate + 2) % 4, (wg_ss, wg_rs), dev(z, chip_mate))

    for d in (1, 3, 2):
        for yr in range(2):
            w_copy(d, yr).start()

    for h in range(HEADS):
        for a in range(3):
            loads[h][a].wait()
            source = QA[h] if a == 0 else KV[h, a - 1, ROWS:, :]
            TMP[a] = source.astype(f32)
            SM[h, a] = TMP[a, pl.ds(h, 256, stride=4), :].astype(bf16)
            SF[h, a] = TMP[a, pl.ds(4 * x + h, 64, stride=16), :].astype(bf16)

    def plane_copy(d, kind):
        s = plane_peer(d)
        return plane_descriptor(d, kind, s, i, s)

    def plane_arrived(d, kind):
        s = (i + 4 - d) % 4
        return plane_descriptor(d, kind, s, s, i)

    def plane_descriptor(d, kind, target, sender, slot):
        mid = pl.multiple_of(sender * 256, 256)
        far = pl.multiple_of(sender * 64, 64)
        src, dst = (
            (SF.at[slot, pl.ds(1, 2)], FKV.at[z, :, pl.ds(far, 64)]),
            (SF.at[slot, 0], FQ.at[pl.ds(far, 64)]),
            (SM.at[slot, pl.ds(1, 2)], KV.at[4, :, pl.ds(ROWS + mid, 256)]),
            (SM.at[slot, 0], QA.at[4, pl.ds(mid, 256)]),
        )[kind]
        return pltpu.make_async_remote_copy(
            src, dst, p_ss.at[d - 1, kind], p_rs.at[d - 1, kind],
            device_id=dev(z, target), device_id_type=MESH)

    def cross_query(s, sender):
        return pltpu.make_async_remote_copy(
            SM.at[s, 0], CQ.at[pl.ds(pl.multiple_of(sender * 256, 256), 256)],
            cq_ss.at[s], cq_rs.at[sender], device_id=dev(pair, s), device_id_type=MESH)

    for kind in (0, 1):
        for d in (2, 3, 1):
            plane_copy(d, kind).start()

    for kind in (2, 3):
        for d in (2, 3, 1):
            plane_copy(d, kind).start()

    @pl.when(zpar == 1)
    def _():
        for s in range(4):
            cross_query(s, i).start()

    own_mid = pl.multiple_of(i * 256, 256)
    own_far = pl.multiple_of(i * 64, 64)
    QA[4, pl.ds(own_mid, 256), :] = SM[i, 0]
    FQ[pl.ds(own_far, 64), :] = SF[i, 0]
    for a in range(2):
        KV[4, a, pl.ds(ROWS + own_mid, 256), :] = SM[i, 1 + a]
        FKV[z, a, pl.ds(own_far, 64), :] = SF[i, 1 + a]

    def forward(hop, slot):
        return pltpu.make_async_remote_copy(
            FKV.at[slot], FKV.at[slot], f_ss.at[hop], f_rs.at[hop],
            device_id=dev(znext, i), device_id_type=MESH)

    def backward(hop, slot):
        return pltpu.make_async_remote_copy(
            FKV.at[slot], FKV.at[slot], b_ss.at[hop], b_rs.at[hop],
            device_id=dev(zprev, i), device_id_type=MESH)

    def tiles(h, with_prev):
        for b in range(ROWS // TILE):
            rows = slice(b * TILE, (b + 1) * TILE)
            pieces = []
            if with_prev:
                pieces.append((KV[h, 0, :ROWS, :], KV[h, 1, :ROWS, :], None))
            if b:
                pieces.append((KV[h, 0, ROWS:ROWS + b * TILE, :], KV[h, 1, ROWS:ROWS + b * TILE, :], None))
            diag = slice(ROWS + b * TILE, ROWS + (b + 1) * TILE)
            pieces.append((KV[h, 0, diag, :], KV[h, 1, diag, :], 0))
            numer, peak, total = softmax_pieces(QA[h, rows, :], pieces)
            ACC[h, rows, :] = numer
            PK[h, rows, :] = peak
            TT[h, rows, :] = total

    def x_copy(part, sem):
        return (
            pltpu.make_async_remote_copy(
                AG.at[(0,) + part], AG.at[(1,) + part], ar_ss.at[sem], ar_rs.at[sem],
                device_id=right, device_id_type=MESH),
            pltpu.make_async_remote_copy(
                AG.at[(0,) + part], AG.at[(3,) + part], al_ss.at[sem], al_rs.at[sem],
                device_id=left, device_id_type=MESH),
        )

    def x_relay(part, sem):
        top = part + (pl.ds(0, 128),)
        low = part + (pl.ds(128, 128),)
        return (
            pltpu.make_async_remote_copy(
                AG.at[(1,) + top], AG.at[(2,) + top], or_ss.at[sem], or_rs.at[sem],
                device_id=right, device_id_type=MESH),
            pltpu.make_async_remote_copy(
                AG.at[(3,) + low], AG.at[(2,) + low], ol_ss.at[sem], ol_rs.at[sem],
                device_id=left, device_id_type=MESH),
        )

    def x_pass_on(part, sem):
        for arrived, onward in zip(x_copy(part, sem), x_relay(part, sem)):
            arrived.wait_recv()
            onward.start()

    def near_part(h):
        return (h, pl.ds(1, 3))

    def strided_part(h):
        return (h, 0)

    nfwd = planes // 2
    nbwd = planes - 1 - nfwd

    def level_step(h, carry):
        @pl.when((h < 4) & (core == 1))
        def _():
            for a in range(2):
                pltpu.make_async_remote_copy(
                    KV.at[h, a, pl.ds(0, ROWS)], KV.at[h, a, pl.ds(0, ROWS)], n_ss.at[h, a], n_rs.at[h, a],
                    device_id=dev(z, i + 1 - 2 * core), device_id_type=MESH).wait_recv()

        @pl.when(h == 4)
        def _():
            for kind in (2, 3):
                for d in (1, 2, 3):
                    plane_arrived(d, kind).wait_recv()

        parity = jnp.where(h < 4, core, 0)

        @pl.when(parity == 1)
        def _():
            tiles(h, True)

        @pl.when(parity == 0)
        def _():
            tiles(h, False)

        @pl.when(h == 0)
        def _():
            for kind in (0, 1):
                for d in (1, 2, 3):
                    plane_arrived(d, kind).wait_recv()

        @pl.when(h == 4)
        def _():
            for early in range(2):
                x_pass_on(near_part(early), early)

        @pl.when((h >= 1) & (h <= nfwd))
        def _():
            forward(h - 1, (z + planes - h) % planes).wait_recv()

        @pl.when((h >= 1) & (h <= nbwd))
        def _():
            backward(h - 1, (z + h) % planes).wait_recv()

        @pl.when(h < nfwd)
        def _():
            forward(h, (z + planes - h) % planes).start()

        @pl.when(h < nbwd)
        def _():
            backward(h, (z + h) % planes).start()

        @pl.when(h < 4)
        def _():
            for rr in range(1, 4):
                picked = (h, pl.ds((h + rr) % 4, 256, stride=4), slice(None))
                AG[0, h, rr] = (ACC[picked] / TT[picked]).astype(bf16)
            for copy in x_copy(near_part(h), h):
                copy.start()

        @pl.when(h == 2)
        def _():
            for d in (1, 3, 2):
                for yr in range(2):
                    w_arrived(d, yr).wait_recv()
                    w_cross(d, yr).start()
                    w_chip(d, yr).start()

        return carry

    lax.fori_loop(0, HEADS + 1, level_step, 0)

    lane = lax.broadcasted_iota(jnp.int32, (256, DH), 1)

    def pack(slot, numer, peak, total):
        OB[slot] = (numer / total).astype(bf16)
        ST[slot] = jnp.transpose(jnp.where(lane == 0, peak, total))[:8, :]

    def cross_result(s, sender, kind):
        src, dst = ((OB, RO), (ST, RST))[kind]
        return pltpu.make_async_remote_copy(
            src.at[4 + s], dst.at[4 + sender], cr_ss.at[s, kind], cr_rs.at[sender, kind],
            device_id=dev(pair, s), device_id_type=MESH)

    @pl.when(zpar == 0)
    def _():
        for s in range(4):
            cross_query(s, s).wait_recv()
            rows = slice(s * 256, (s + 1) * 256)
            pack(4 + s, *softmax_pieces(CQ[rows, :], [(KV[4, 0, ROWS:, :], KV[4, 1, ROWS:, :], None)]))
            for kind in range(2):
                cross_result(s, i, kind).start()

    far_pieces = [(FKV[j, 0], FKV[j, 1], TILE * (z - j)) for j in range(planes)]
    far = softmax_pieces(FQ[...], far_pieces)
    picked = (4, pl.ds(x, 256, stride=4), slice(None))
    mid = (ACC[picked], PK[picked], TT[picked])
    ACC[picked], PK[picked], TT[picked] = merge(mid, far)
    for s in range(4):
        rows = slice(s * 256, (s + 1) * 256)
        pack(s, ACC[4, rows, :], PK[4, rows, :], TT[4, rows, :])

    def back_copy(d, kind):
        s = plane_peer(d)
        src, dst = ((OB, RO), (ST, RST))[kind]
        return pltpu.make_async_remote_copy(
            src.at[s], dst.at[i], r_ss.at[d - 1, kind], r_rs.at[d - 1, kind],
            device_id=dev(z, s), device_id_type=MESH)

    def back_arrived(d, kind):
        s = (i + 4 - d) % 4
        src, dst = ((OB, RO), (ST, RST))[kind]
        return pltpu.make_async_remote_copy(
            src.at[i], dst.at[s], r_ss.at[d - 1, kind], r_rs.at[d - 1, kind],
            device_id=dev(z, s), device_id_type=MESH)

    for d in (2, 3, 1):
        for kind in range(2):
            back_copy(d, kind).start()
    RO[i] = OB[i]
    RST[i] = ST[i]

    for late in (2, 3):
        x_pass_on(near_part(late), late)

    for d in (1, 3, 2):
        for yr in range(2):
            w_crossed(d, yr).wait_recv()
            w_last(d, yr).start()

    for d in (1, 2, 3):
        for yr in range(2):
            w_chipped(d, yr).wait_recv()
            w_lasted(d, yr).wait_recv()
    for yr in range(2):
        w_own(yr).wait()

    def weight(yr, j, h):
        return WG[yr, (x + 4 - j) % 4, h * DH:(h + 1) * DH, :]

    def product(r, yr, blocks):
        left_side = jnp.concatenate([AG[j, h, (r - h) % 4] for j, h in blocks], axis=1)
        right_side = jnp.concatenate([weight(yr, j, h) for j, h in blocks], axis=0)
        return jnp.dot(left_side, right_side, preferred_element_type=f32)

    for r in range(4):
        blocks = [(j, h) for j in (0, 1, 3) for h in range(HEADS) if h != r]
        for yr, acc in ((1, OTH), (0, OWN)):
            acc[r] = product(r, yr, blocks)

    for d in (1, 2, 3):
        for kind in range(2):
            back_arrived(d, kind).wait_recv()

    @pl.when(zpar == 1)
    def _():
        for s in range(4):
            for kind in range(2):
                cross_result(s, s, kind).wait_recv()

    def unpack(slot):
        stats = jnp.transpose(RST[slot])
        peak = jnp.broadcast_to(stats[:, 0:1], (256, DH))
        total = jnp.broadcast_to(stats[:, 1:2], (256, DH))
        return RO[slot].astype(f32) * total, peak, total

    for s in range(HEADS):
        picked = (s, pl.ds(s, 256, stride=4), slice(None))
        state = merge((ACC[picked], PK[picked], TT[picked]), unpack(s))

        @pl.when(zpar == 0)
        def _():
            AG[0, s, 0] = (state[0] / state[2]).astype(bf16)

        @pl.when(zpar == 1)
        def _():
            numer, _, total = merge(state, unpack(4 + s))
            AG[0, s, 0] = (numer / total).astype(bf16)

        for copy in x_copy(strided_part(s), 4 + s):
            copy.start()

    def to_across(r):
        return pltpu.make_async_remote_copy(
            PS.at[r], PR.at[r], y_ss.at[r], y_rs.at[r], device_id=across, device_id_type=MESH)

    def finish(r):
        for copy in x_relay(strided_part(r), 4 + r):
            copy.wait_recv()
        blocks = [(2, h) for h in range(HEADS) if h != r] + [(j, r) for j in range(4)]
        PS[r] = (OTH[r] + product(r, 1, blocks)).astype(bf16)
        to_across(r).start()
        OWN[r] = OWN[r] + product(r, 0, blocks)

    for r in range(4):
        x_pass_on(strided_part(r), 4 + r)
        if r == 0:
            for h in range(HEADS):
                for copy in x_relay(near_part(h), h):
                    copy.wait_recv()
        else:
            finish(r - 1)
    finish(3)

    for r in range(4):
        to_across(r).wait_recv()
        mixed = OWN[r] + PR[r].astype(f32)
        for c in range(4):
            ACC[c, pl.ds(r, 256, stride=4), :] = mixed[:, c * DH:(c + 1) * DH]
    for c in range(4):
        out_ref[:, c * DH:(c + 1) * DH] = ACC[c].astype(bf16)

    for d in (1, 2, 3):
        for yr in range(2):
            w_copy(d, yr).wait_send()
            w_cross(d, yr).wait_send()
            w_chip(d, yr).wait_send()
            w_last(d, yr).wait_send()
        for kind in range(4):
            plane_copy(d, kind).wait_send()
        for kind in range(2):
            back_copy(d, kind).wait_send()
    for hop in range(nfwd):
        forward(hop, (z + planes - hop) % planes).wait_send()
    for hop in range(nbwd):
        backward(hop, (z + hop) % planes).wait_send()
    for h in range(HEADS):
        for part, sem in ((near_part(h), h), (strided_part(h), 4 + h)):
            for copy in x_copy(part, sem) + x_relay(part, sem):
                copy.wait_send()
        to_across(h).wait_send()

    @pl.when(zpar == 1)
    def _():
        for s in range(4):
            cross_query(s, i).wait_send()

    @pl.when(zpar == 0)
    def _():
        for s in range(4):
            for kind in range(2):
                cross_result(s, i, kind).wait_send()

    @pl.when(core == 0)
    def _():
        for h in range(HEADS):
            for a in range(2):
                near_copy(h, a).wait_send()


def shards(planes, queries, keys, values, out_weight):
    dma = pltpu.SemaphoreType.DMA
    vmem = pltpu.VMEM
    anywhere = pl.BlockSpec(memory_space=pltpu.HBM)
    return pl.pallas_call(
        functools.partial(layer_kernel, planes),
        name="layer",
        out_shape=jax.ShapeDtypeStruct((ROWS, HEADS * DH), bf16),
        in_specs=[anywhere] * 4,
        out_specs=pl.BlockSpec(memory_space=pltpu.VMEM),
        scratch_shapes=[
            vmem((5, ROWS, DH), bf16),
            vmem((5, 2, 2 * ROWS, DH), bf16),
            vmem((4, 3, 256, DH), bf16),
            vmem((4, 3, 64, DH), bf16),
            vmem((256, DH), bf16),
            vmem((planes, 2, 256, DH), bf16),
            vmem((5, ROWS, DH), f32),
            vmem((5, ROWS, DH), f32),
            vmem((5, ROWS, DH), f32),
            vmem((3, ROWS, DH), f32),
            vmem((8, 256, DH), bf16),
            vmem((8, 8, 256), f32),
            vmem((8, 256, DH), bf16),
            vmem((8, 8, 256), f32),
            vmem((ROWS, DH), bf16),
            vmem((2, 4, 512, 512), bf16),
            vmem((4, 4, 4, 256, DH), bf16),
            vmem((4, 256, 512), bf16),
            vmem((4, 256, 512), bf16),
            vmem((4, 256, 512), f32),
            vmem((4, 256, 512), f32),
            dma((4, 3)), dma((2,)),
            dma((3, 2)), dma((3, 2)), dma((3, 2)), dma((3, 2)),
            dma((3, 2)), dma((3, 2)), dma((3, 2)), dma((3, 2)),
            dma((4, 2)), dma((4, 2)),
            dma((3, 4)), dma((3, 4)),
            dma((4,)), dma((4,)),
            dma((4,)), dma((4,)), dma((4,)), dma((4,)),
            dma((3, 2)), dma((3, 2)),
            dma((4, 2)), dma((4, 2)),
        ] + [dma((8,))] * 8 + [dma((4,))] * 2,
        compiler_params=pltpu.CompilerParams(
            collective_id=0, has_side_effects=True, vmem_limit_bytes=52 * 1024 * 1024),
    )(queries, keys, values, out_weight)


def solution(mesh):
    placed = (P("seq", "head"), P("seq", "head"), P("seq", "head"), P("head", None))
    planes = mesh.shape["seq"] // 4
    return jax.shard_map(
        functools.partial(shards, planes), mesh=mesh, in_specs=placed, out_specs=P("seq", "head"), check_vma=False
    )
```

```python
import functools
import math

import jax
import jax.numpy as jnp
from jax import lax
from jax.experimental import pallas as pl
from jax.experimental.pallas import tpu as pltpu
from jax.sharding import PartitionSpec as P

DH = 128
ROWS = 1024
HEADS = 4
TILE = 256
NEG = -1e30
SCALE2 = math.log2(math.e) / math.sqrt(DH)
MESH = pl.DeviceIdType.MESH
bf16 = jnp.bfloat16
f32 = jnp.float32


def nt_dot(a, b):
    return lax.dot_general(a, b, (((1,), (1,)), ((), ())), preferred_element_type=f32)


def softmax_pieces(query, pieces):
    scores = []
    for key_rows, _, limit in pieces:
        score = nt_dot(query, key_rows)
        if limit is not None:
            row = lax.broadcasted_iota(jnp.int32, score.shape, 0)
            col = lax.broadcasted_iota(jnp.int32, score.shape, 1)
            score = jnp.where(col - row <= limit, score, NEG)
        scores.append(score)
    peak = functools.reduce(jnp.maximum, [jnp.max(s, axis=1, keepdims=True) for s in scores])
    both = None
    for score, (_, value_rows, _) in zip(scores, pieces):
        weights = jnp.exp2((score - peak) * SCALE2).astype(bf16)
        ones = jnp.ones(value_rows.shape, bf16)
        term = jnp.dot(weights, jnp.concatenate([value_rows, ones], axis=1), preferred_element_type=f32)
        both = term if both is None else both + term
    numer, total = both[:, :DH], both[:, DH:]
    return numer, jnp.broadcast_to(peak, numer.shape), total


def merge(one, two):
    numer1, peak1, total1 = one
    numer2, peak2, total2 = two
    top = jnp.maximum(peak1, peak2)
    f1 = jnp.exp2((peak1 - top) * SCALE2)
    f2 = jnp.exp2((peak2 - top) * SCALE2)
    return numer1 * f1 + numer2 * f2, top, total1 * f1 + total2 * f2


def layer_kernel(
    planes,
    q_hbm, k_hbm, v_hbm, w_hbm, out_ref,
    QA, KV, SM, SF, FQ, FKV, ACC, PK, TT, TMP, RO, RST, OB, ST, CQ, WG, AG, PS, PR, OWN, OTH,
    loc, locw, w_ss, w_rs, wy_ss, wy_rs, wf_ss, wf_rs, wg_ss, wg_rs, n_ss, n_rs, p_ss, p_rs, cq_ss, cq_rs,
    f_ss, f_rs, b_ss, b_rs, r_ss, r_rs, cr_ss, cr_rs,
    ar_ss, ar_rs, al_ss, al_rs, or_ss, or_rs, ol_ss, ol_rs, y_ss, y_rs,
):
    seq = lax.axis_index("seq")
    head = lax.axis_index("head")
    z = seq // 4
    i = seq % 4
    core = seq % 2
    zpar = z % 2
    x = head % 4
    y = head // 4

    def dev(plane, slot):
        return (plane * 4 + slot, head)

    def plane_peer(d):
        return (i + d) % 4

    pair = z + 1 - 2 * zpar
    znext = (z + 1) % planes
    zprev = (z + planes - 1) % planes
    zother = (z + planes - 1 + 2 * zpar) % planes

    loads = []
    for h in range(HEADS):
        cols = slice(h * DH, (h + 1) * DH)
        loads.append([
            pltpu.make_async_copy(q_hbm.at[:, cols], QA.at[h], loc.at[h, 0]),
            pltpu.make_async_copy(k_hbm.at[:, cols], KV.at[h, 0, pl.ds(ROWS, ROWS)], loc.at[h, 1]),
            pltpu.make_async_copy(v_hbm.at[:, cols], KV.at[h, 1, pl.ds(ROWS, ROWS)], loc.at[h, 2]),
        ])
        for copy in loads[-1]:
            copy.start()

    def w_own(yr):
        col = pl.multiple_of((((y + yr) % 2) * 4 + x) * 512, 512)
        return pltpu.make_async_copy(w_hbm.at[:, pl.ds(col, 512)], WG.at[yr, x], locw.at[yr])

    for yr in range(2):
        w_own(yr).start()

    barrier = pltpu.get_barrier_semaphore()
    greet = [dev(z, plane_peer(d)) for d in (1, 2, 3)]
    greet += [dev(pair, s) for s in range(4)]
    greet += [dev(zother, i)]
    greet += [(seq, y * 4 + (x + d) % 4) for d in (1, 2, 3)]
    right = (seq, y * 4 + (x + 1) % 4)
    left = (seq, y * 4 + (x + 3) % 4)
    across = (seq, (1 - y) * 4 + x)
    greet += [across]
    for target in greet:
        pl.semaphore_signal(barrier, inc=1, device_id=target, device_id_type=MESH)
    pl.semaphore_wait(barrier, len(greet))

    def near_copy(h, a):
        src = (k_hbm, v_hbm)[a].at[:, h * DH:(h + 1) * DH]
        return pltpu.make_async_remote_copy(
            src, KV.at[h, a, pl.ds(0, ROWS)], n_ss.at[h, a], n_rs.at[h, a],
            device_id=dev(z, i + 1 - 2 * core), device_id_type=MESH)

    @pl.when(core == 0)
    def _():
        for h in range(HEADS):
            for a in range(2):
                near_copy(h, a).start()

    chip_mate = i + 1 - 2 * core
    y_mate = (i + 2) % 4

    def quarter(slot):
        return pl.ds(pl.multiple_of(slot * 128, 128), 128)

    def w_copy(d, yr):
        xd = (x + d) % 4
        yd = (y + yr) % 2
        col = pl.multiple_of((yd * 4 + xd) * 512, 512)
        return pltpu.make_async_remote_copy(
            w_hbm.at[quarter(i), pl.ds(col, 512)], WG.at[yr, x, quarter(i)],
            w_ss.at[d - 1, yr], w_rs.at[d - 1, yr],
            device_id=(seq, y * 4 + xd), device_id_type=MESH)

    def w_share(d, yr, slot, sems, target):
        piece = WG.at[yr, (x + 4 - d) % 4, quarter(slot)]
        return pltpu.make_async_remote_copy(
            piece, piece, sems[0].at[d - 1, yr], sems[1].at[d - 1, yr],
            device_id=target, device_id_type=MESH)

    def w_arrived(d, yr):
        return w_share(d, yr, i, (w_ss, w_rs), (seq, y * 4 + (x + 4 - d) % 4))

    def w_cross(d, yr):
        return w_share(d, yr, i, (wy_ss, wy_rs), dev(z, y_mate))

    def w_crossed(d, yr):
        return w_share(d, yr, y_mate, (wy_ss, wy_rs), dev(z, y_mate))

    def w_chip(d, yr):
        return w_share(d, yr, i, (wf_ss, wf_rs), dev(z, chip_mate))

    def w_chipped(d, yr):
        return w_share(d, yr, chip_mate, (wf_ss, wf_rs), dev(z, chip_mate))

    def w_last(d, yr):
        return w_share(d, yr, y_mate, (wg_ss, wg_rs), dev(z, chip_mate))

    def w_lasted(d, yr):
        return w_share(d, yr, (chip_mate + 2) % 4, (wg_ss, wg_rs), dev(z, chip_mate))

    for d in (1, 3, 2):
        for yr in range(2):
            w_copy(d, yr).start()

    for h in range(HEADS):
        for a in range(3):
            loads[h][a].wait()
            source = QA[h] if a == 0 else KV[h, a - 1, ROWS:, :]
            TMP[a] = source.astype(f32)
            SM[h, a] = TMP[a, pl.ds(h, 256, stride=4), :].astype(bf16)
            SF[h, a] = TMP[a, pl.ds(4 * x + h, 64, stride=16), :].astype(bf16)

    def plane_copy(d, kind):
        s = plane_peer(d)
        return plane_descriptor(d, kind, s, i, s)

    def plane_arrived(d, kind):
        s = (i + 4 - d) % 4
        return plane_descriptor(d, kind, s, s, i)

    def plane_descriptor(d, kind, target, sender, slot):
        mid = pl.multiple_of(sender * 256, 256)
        far = pl.multiple_of(sender * 64, 64)
        src, dst = (
            (SF.at[slot, pl.ds(1, 2)], FKV.at[z, :, pl.ds(far, 64)]),
            (SF.at[slot, 0], FQ.at[pl.ds(far, 64)]),
            (SM.at[slot, pl.ds(1, 2)], KV.at[4, :, pl.ds(ROWS + mid, 256)]),
            (SM.at[slot, 0], QA.at[4, pl.ds(mid, 256)]),
        )[kind]
        return pltpu.make_async_remote_copy(
            src, dst, p_ss.at[d - 1, kind], p_rs.at[d - 1, kind],
            device_id=dev(z, target), device_id_type=MESH)

    def cross_query(s, sender):
        return pltpu.make_async_remote_copy(
            SM.at[s, 0], CQ.at[pl.ds(pl.multiple_of(sender * 256, 256), 256)],
            cq_ss.at[s], cq_rs.at[sender], device_id=dev(pair, s), device_id_type=MESH)

    for kind in (0, 1):
        for d in (2, 3, 1):
            plane_copy(d, kind).start()

    for kind in (2, 3):
        for d in (2, 3, 1):
            plane_copy(d, kind).start()

    @pl.when(zpar == 1)
    def _():
        for s in range(4):
            cross_query(s, i).start()

    own_mid = pl.multiple_of(i * 256, 256)
    own_far = pl.multiple_of(i * 64, 64)
    QA[4, pl.ds(own_mid, 256), :] = SM[i, 0]
    FQ[pl.ds(own_far, 64), :] = SF[i, 0]
    for a in range(2):
        KV[4, a, pl.ds(ROWS + own_mid, 256), :] = SM[i, 1 + a]
        FKV[z, a, pl.ds(own_far, 64), :] = SF[i, 1 + a]

    def forward(hop, slot):
        return pltpu.make_async_remote_copy(
            FKV.at[slot], FKV.at[slot], f_ss.at[hop], f_rs.at[hop],
            device_id=dev(znext, i), device_id_type=MESH)

    def backward(hop, slot):
        return pltpu.make_async_remote_copy(
            FKV.at[slot], FKV.at[slot], b_ss.at[hop], b_rs.at[hop],
            device_id=dev(zprev, i), device_id_type=MESH)

    def tiles(h, with_prev):
        for b in range(ROWS // TILE):
            rows = slice(b * TILE, (b + 1) * TILE)
            pieces = []
            if with_prev:
                pieces.append((KV[h, 0, :ROWS, :], KV[h, 1, :ROWS, :], None))
            if b:
                pieces.append((KV[h, 0, ROWS:ROWS + b * TILE, :], KV[h, 1, ROWS:ROWS + b * TILE, :], None))
            diag = slice(ROWS + b * TILE, ROWS + (b + 1) * TILE)
            pieces.append((KV[h, 0, diag, :], KV[h, 1, diag, :], 0))
            numer, peak, total = softmax_pieces(QA[h, rows, :], pieces)
            ACC[h, rows, :] = numer
            PK[h, rows, :] = peak
            TT[h, rows, :] = total

    def x_copy(part, sem):
        return (
            pltpu.make_async_remote_copy(
                AG.at[(0,) + part], AG.at[(1,) + part], ar_ss.at[sem], ar_rs.at[sem],
                device_id=right, device_id_type=MESH),
            pltpu.make_async_remote_copy(
                AG.at[(0,) + part], AG.at[(3,) + part], al_ss.at[sem], al_rs.at[sem],
                device_id=left, device_id_type=MESH),
        )

    def x_relay(part, sem):
        top = part + (pl.ds(0, 128),)
        low = part + (pl.ds(128, 128),)
        return (
            pltpu.make_async_remote_copy(
                AG.at[(1,) + top], AG.at[(2,) + top], or_ss.at[sem], or_rs.at[sem],
                device_id=right, device_id_type=MESH),
            pltpu.make_async_remote_copy(
                AG.at[(3,) + low], AG.at[(2,) + low], ol_ss.at[sem], ol_rs.at[sem],
                device_id=left, device_id_type=MESH),
        )

    def x_pass_on(part, sem):
        for arrived, onward in zip(x_copy(part, sem), x_relay(part, sem)):
            arrived.wait_recv()
            onward.start()

    def near_part(h):
        return (h, pl.ds(1, 3))

    def strided_part(h):
        return (h, 0)

    nfwd = planes // 2
    nbwd = planes - 1 - nfwd

    def level_step(h, carry):
        @pl.when((h < 4) & (core == 1))
        def _():
            for a in range(2):
                pltpu.make_async_remote_copy(
                    KV.at[h, a, pl.ds(0, ROWS)], KV.at[h, a, pl.ds(0, ROWS)], n_ss.at[h, a], n_rs.at[h, a],
                    device_id=dev(z, i + 1 - 2 * core), device_id_type=MESH).wait_recv()

        @pl.when(h == 4)
        def _():
            for kind in (2, 3):
                for d in (1, 2, 3):
                    plane_arrived(d, kind).wait_recv()

        parity = jnp.where(h < 4, core, 0)

        @pl.when(parity == 1)
        def _():
            tiles(h, True)

        @pl.when(parity == 0)
        def _():
            tiles(h, False)

        @pl.when(h == 0)
        def _():
            for kind in (0, 1):
                for d in (1, 2, 3):
                    plane_arrived(d, kind).wait_recv()

        @pl.when(h == 4)
        def _():
            for early in range(2):
                x_pass_on(near_part(early), early)

        @pl.when((h >= 1) & (h <= nfwd))
        def _():
            forward(h - 1, (z + planes - h) % planes).wait_recv()

        @pl.when((h >= 1) & (h <= nbwd))
        def _():
            backward(h - 1, (z + h) % planes).wait_recv()

        @pl.when(h < nfwd)
        def _():
            forward(h, (z + planes - h) % planes).start()

        @pl.when(h < nbwd)
        def _():
            backward(h, (z + h) % planes).start()

        @pl.when(h < 4)
        def _():
            for rr in range(1, 4):
                picked = (h, pl.ds((h + rr) % 4, 256, stride=4), slice(None))
                AG[0, h, rr] = (ACC[picked] / TT[picked]).astype(bf16)
            for copy in x_copy(near_part(h), h):
                copy.start()

        @pl.when(h == 3)
        def _():
            for d in (1, 3, 2):
                for yr in range(2):
                    w_arrived(d, yr).wait_recv()
                    w_cross(d, yr).start()
                    w_chip(d, yr).start()

        return carry

    lax.fori_loop(0, HEADS + 1, level_step, 0)

    lane = lax.broadcasted_iota(jnp.int32, (256, DH), 1)

    def pack(slot, numer, peak, total):
        OB[slot] = (numer / total).astype(bf16)
        ST[slot] = jnp.transpose(jnp.where(lane == 0, peak, total))[:8, :]

    def cross_result(s, sender, kind):
        src, dst = ((OB, RO), (ST, RST))[kind]
        return pltpu.make_async_remote_copy(
            src.at[4 + s], dst.at[4 + sender], cr_ss.at[s, kind], cr_rs.at[sender, kind],
            device_id=dev(pair, s), device_id_type=MESH)

    @pl.when(zpar == 0)
    def _():
        for s in range(4):
            cross_query(s, s).wait_recv()
            rows = slice(s * 256, (s + 1) * 256)
            pack(4 + s, *softmax_pieces(CQ[rows, :], [(KV[4, 0, ROWS:, :], KV[4, 1, ROWS:, :], None)]))
            for kind in range(2):
                cross_result(s, i, kind).start()

    far_pieces = [(FKV[j, 0], FKV[j, 1], TILE * (z - j)) for j in range(planes)]
    far = softmax_pieces(FQ[...], far_pieces)
    picked = (4, pl.ds(x, 256, stride=4), slice(None))
    mid = (ACC[picked], PK[picked], TT[picked])
    ACC[picked], PK[picked], TT[picked] = merge(mid, far)
    for s in range(4):
        rows = slice(s * 256, (s + 1) * 256)
        pack(s, ACC[4, rows, :], PK[4, rows, :], TT[4, rows, :])

    def back_copy(d, kind):
        s = plane_peer(d)
        src, dst = ((OB, RO), (ST, RST))[kind]
        return pltpu.make_async_remote_copy(
            src.at[s], dst.at[i], r_ss.at[d - 1, kind], r_rs.at[d - 1, kind],
            device_id=dev(z, s), device_id_type=MESH)

    def back_arrived(d, kind):
        s = (i + 4 - d) % 4
        src, dst = ((OB, RO), (ST, RST))[kind]
        return pltpu.make_async_remote_copy(
            src.at[i], dst.at[s], r_ss.at[d - 1, kind], r_rs.at[d - 1, kind],
            device_id=dev(z, s), device_id_type=MESH)

    for d in (2, 3, 1):
        for kind in range(2):
            back_copy(d, kind).start()
    RO[i] = OB[i]
    RST[i] = ST[i]

    for late in (2, 3):
        x_pass_on(near_part(late), late)

    for d in (1, 3, 2):
        for yr in range(2):
            w_crossed(d, yr).wait_recv()
            w_last(d, yr).start()

    for d in (1, 2, 3):
        for kind in range(2):
            back_arrived(d, kind).wait_recv()

    @pl.when(zpar == 1)
    def _():
        for s in range(4):
            for kind in range(2):
                cross_result(s, s, kind).wait_recv()

    def unpack(slot):
        stats = jnp.transpose(RST[slot])
        peak = jnp.broadcast_to(stats[:, 0:1], (256, DH))
        total = jnp.broadcast_to(stats[:, 1:2], (256, DH))
        return RO[slot].astype(f32) * total, peak, total

    for s in range(HEADS):
        picked = (s, pl.ds(s, 256, stride=4), slice(None))
        state = merge((ACC[picked], PK[picked], TT[picked]), unpack(s))

        @pl.when(zpar == 0)
        def _():
            AG[0, s, 0] = (state[0] / state[2]).astype(bf16)

        @pl.when(zpar == 1)
        def _():
            numer, _, total = merge(state, unpack(4 + s))
            AG[0, s, 0] = (numer / total).astype(bf16)

        for copy in x_copy(strided_part(s), 4 + s):
            copy.start()

    def weight(yr, j, h):
        return WG[yr, (x + 4 - j) % 4, h * DH:(h + 1) * DH, :]

    def product(r, yr, blocks):
        left_side = jnp.concatenate([AG[j, h, (r - h) % 4] for j, h in blocks], axis=1)
        right_side = jnp.concatenate([weight(yr, j, h) for j, h in blocks], axis=0)
        return jnp.dot(left_side, right_side, preferred_element_type=f32)

    def to_across(r):
        return pltpu.make_async_remote_copy(
            PS.at[r], PR.at[r], y_ss.at[r], y_rs.at[r], device_id=across, device_id_type=MESH)

    def finish(r):
        for copy in x_relay(strided_part(r), 4 + r):
            copy.wait_recv()
        blocks = [(2, h) for h in range(HEADS) if h != r] + [(j, r) for j in range(4)]
        PS[r] = (OTH[r] + product(r, 1, blocks)).astype(bf16)
        to_across(r).start()
        OWN[r] = OWN[r] + product(r, 0, blocks)

    def begin(r):
        blocks = [(j, h) for j in (0, 1, 3) for h in range(HEADS) if h != r]
        for yr, acc in ((1, OTH), (0, OWN)):
            acc[r] = product(r, yr, blocks)

    for d in (1, 2, 3):
        for yr in range(2):
            w_chipped(d, yr).wait_recv()
            w_lasted(d, yr).wait_recv()
    for yr in range(2):
        w_own(yr).wait()

    begin(0)
    for r in range(4):
        x_pass_on(strided_part(r), 4 + r)
        if r == 0:
            for h in range(HEADS):
                for copy in x_relay(near_part(h), h):
                    copy.wait_recv()
        else:
            finish(r - 1)
        if r < 3:
            begin(r + 1)
    finish(3)

    for r in range(4):
        to_across(r).wait_recv()
        mixed = OWN[r] + PR[r].astype(f32)
        for c in range(4):
            ACC[c, pl.ds(r, 256, stride=4), :] = mixed[:, c * DH:(c + 1) * DH]
    for c in range(4):
        out_ref[:, c * DH:(c + 1) * DH] = ACC[c].astype(bf16)

    for d in (1, 2, 3):
        for yr in range(2):
            w_copy(d, yr).wait_send()
            w_cross(d, yr).wait_send()
            w_chip(d, yr).wait_send()
            w_last(d, yr).wait_send()
        for kind in range(4):
            plane_copy(d, kind).wait_send()
        for kind in range(2):
            back_copy(d, kind).wait_send()
    for hop in range(nfwd):
        forward(hop, (z + planes - hop) % planes).wait_send()
    for hop in range(nbwd):
        backward(hop, (z + hop) % planes).wait_send()
    for h in range(HEADS):
        for part, sem in ((near_part(h), h), (strided_part(h), 4 + h)):
            for copy in x_copy(part, sem) + x_relay(part, sem):
                copy.wait_send()
        to_across(h).wait_send()

    @pl.when(zpar == 1)
    def _():
        for s in range(4):
            cross_query(s, i).wait_send()

    @pl.when(zpar == 0)
    def _():
        for s in range(4):
            for kind in range(2):
                cross_result(s, i, kind).wait_send()

    @pl.when(core == 0)
    def _():
        for h in range(HEADS):
            for a in range(2):
                near_copy(h, a).wait_send()


def shards(planes, queries, keys, values, out_weight):
    dma = pltpu.SemaphoreType.DMA
    vmem = pltpu.VMEM
    anywhere = pl.BlockSpec(memory_space=pltpu.HBM)
    return pl.pallas_call(
        functools.partial(layer_kernel, planes),
        name="layer",
        out_shape=jax.ShapeDtypeStruct((ROWS, HEADS * DH), bf16),
        in_specs=[anywhere] * 4,
        out_specs=pl.BlockSpec(memory_space=pltpu.VMEM),
        scratch_shapes=[
            vmem((5, ROWS, DH), bf16),
            vmem((5, 2, 2 * ROWS, DH), bf16),
            vmem((4, 3, 256, DH), bf16),
            vmem((4, 3, 64, DH), bf16),
            vmem((256, DH), bf16),
            vmem((planes, 2, 256, DH), bf16),
            vmem((5, ROWS, DH), f32),
            vmem((5, ROWS, DH), f32),
            vmem((5, ROWS, DH), f32),
            vmem((3, ROWS, DH), f32),
            vmem((8, 256, DH), bf16),
            vmem((8, 8, 256), f32),
            vmem((8, 256, DH), bf16),
            vmem((8, 8, 256), f32),
            vmem((ROWS, DH), bf16),
            vmem((2, 4, 512, 512), bf16),
            vmem((4, 4, 4, 256, DH), bf16),
            vmem((4, 256, 512), bf16),
            vmem((4, 256, 512), bf16),
            vmem((4, 256, 512), f32),
            vmem((4, 256, 512), f32),
            dma((4, 3)), dma((2,)),
            dma((3, 2)), dma((3, 2)), dma((3, 2)), dma((3, 2)),
            dma((3, 2)), dma((3, 2)), dma((3, 2)), dma((3, 2)),
            dma((4, 2)), dma((4, 2)),
            dma((3, 4)), dma((3, 4)),
            dma((4,)), dma((4,)),
            dma((4,)), dma((4,)), dma((4,)), dma((4,)),
            dma((3, 2)), dma((3, 2)),
            dma((4, 2)), dma((4, 2)),
        ] + [dma((8,))] * 8 + [dma((4,))] * 2,
        compiler_params=pltpu.CompilerParams(
            collective_id=0, has_side_effects=True, vmem_limit_bytes=52 * 1024 * 1024),
    )(queries, keys, values, out_weight)


def solution(mesh):
    placed = (P("seq", "head"), P("seq", "head"), P("seq", "head"), P("head", None))
    planes = mesh.shape["seq"] // 4
    return jax.shard_map(
        functools.partial(shards, planes), mesh=mesh, in_specs=placed, out_specs=P("seq", "head"), check_vma=False
    )
```

```python
import functools
import math

import jax
import jax.numpy as jnp
from jax import lax
from jax.experimental import pallas as pl
from jax.experimental.pallas import tpu as pltpu
from jax.sharding import PartitionSpec as P

DH = 128
ROWS = 1024
HEADS = 4
TILE = 256
NEG = -1e30
SCALE2 = math.log2(math.e) / math.sqrt(DH)
MESH = pl.DeviceIdType.MESH
bf16 = jnp.bfloat16
f32 = jnp.float32


def nt_dot(a, b):
    return lax.dot_general(a, b, (((1,), (1,)), ((), ())), preferred_element_type=f32)


def softmax_pieces(query, pieces):
    scores = []
    for key_rows, _, limit in pieces:
        score = nt_dot(query, key_rows)
        if limit is not None:
            row = lax.broadcasted_iota(jnp.int32, score.shape, 0)
            col = lax.broadcasted_iota(jnp.int32, score.shape, 1)
            score = jnp.where(col - row <= limit, score, NEG)
        scores.append(score)
    peak = functools.reduce(jnp.maximum, [jnp.max(s, axis=1, keepdims=True) for s in scores])
    both = None
    for score, (_, value_rows, _) in zip(scores, pieces):
        weights = jnp.exp2((score - peak) * SCALE2).astype(bf16)
        ones = jnp.ones(value_rows.shape, bf16)
        term = jnp.dot(weights, jnp.concatenate([value_rows, ones], axis=1), preferred_element_type=f32)
        both = term if both is None else both + term
    numer, total = both[:, :DH], both[:, DH:]
    return numer, jnp.broadcast_to(peak, numer.shape), total


def merge(one, two):
    numer1, peak1, total1 = one
    numer2, peak2, total2 = two
    top = jnp.maximum(peak1, peak2)
    f1 = jnp.exp2((peak1 - top) * SCALE2)
    f2 = jnp.exp2((peak2 - top) * SCALE2)
    return numer1 * f1 + numer2 * f2, top, total1 * f1 + total2 * f2


def layer_kernel(
    planes,
    q_hbm, k_hbm, v_hbm, w_hbm, out_ref,
    QA, KV, SM, SF, FQ, FKV, ACC, PK, TT, TMP, RO, RST, OB, ST, CQ, WG, AG, PS, PR, OWN, OTH,
    loc, locw, w_ss, w_rs, wy_ss, wy_rs, wf_ss, wf_rs, wg_ss, wg_rs, n_ss, n_rs, p_ss, p_rs, cq_ss, cq_rs,
    f_ss, f_rs, b_ss, b_rs, r_ss, r_rs, cr_ss, cr_rs,
    ar_ss, ar_rs, al_ss, al_rs, or_ss, or_rs, ol_ss, ol_rs, y_ss, y_rs,
):
    seq = lax.axis_index("seq")
    head = lax.axis_index("head")
    z = seq // 4
    i = seq % 4
    core = seq % 2
    zpar = z % 2
    x = head % 4
    y = head // 4

    def dev(plane, slot):
        return (plane * 4 + slot, head)

    def plane_peer(d):
        return (i + d) % 4

    pair = z + 1 - 2 * zpar
    znext = (z + 1) % planes
    zprev = (z + planes - 1) % planes
    zother = (z + planes - 1 + 2 * zpar) % planes

    loads = []
    for h in range(HEADS):
        cols = slice(h * DH, (h + 1) * DH)
        loads.append([
            pltpu.make_async_copy(q_hbm.at[:, cols], QA.at[h], loc.at[h, 0]),
            pltpu.make_async_copy(k_hbm.at[:, cols], KV.at[h, 0, pl.ds(ROWS, ROWS)], loc.at[h, 1]),
            pltpu.make_async_copy(v_hbm.at[:, cols], KV.at[h, 1, pl.ds(ROWS, ROWS)], loc.at[h, 2]),
        ])
        for copy in loads[-1]:
            copy.start()

    def w_own(yr):
        col = pl.multiple_of((((y + yr) % 2) * 4 + x) * 512, 512)
        return pltpu.make_async_copy(w_hbm.at[:, pl.ds(col, 512)], WG.at[yr, x], locw.at[yr])

    for yr in range(2):
        w_own(yr).start()

    barrier = pltpu.get_barrier_semaphore()
    greet = [dev(z, plane_peer(d)) for d in (1, 2, 3)]
    greet += [dev(pair, s) for s in range(4)]
    greet += [dev(zother, i)]
    greet += [(seq, y * 4 + (x + d) % 4) for d in (1, 2, 3)]
    right = (seq, y * 4 + (x + 1) % 4)
    left = (seq, y * 4 + (x + 3) % 4)
    across = (seq, (1 - y) * 4 + x)
    greet += [across]
    for target in greet:
        pl.semaphore_signal(barrier, inc=1, device_id=target, device_id_type=MESH)
    pl.semaphore_wait(barrier, len(greet))

    def near_copy(h, a):
        src = (k_hbm, v_hbm)[a].at[:, h * DH:(h + 1) * DH]
        return pltpu.make_async_remote_copy(
            src, KV.at[h, a, pl.ds(0, ROWS)], n_ss.at[h, a], n_rs.at[h, a],
            device_id=dev(z, i + 1 - 2 * core), device_id_type=MESH)

    @pl.when(core == 0)
    def _():
        for h in range(HEADS):
            for a in range(2):
                near_copy(h, a).start()

    chip_mate = i + 1 - 2 * core
    y_mate = (i + 2) % 4

    def quarter(slot):
        return pl.ds(pl.multiple_of(slot * 128, 128), 128)

    def w_copy(d, yr):
        xd = (x + d) % 4
        yd = (y + yr) % 2
        col = pl.multiple_of((yd * 4 + xd) * 512, 512)
        return pltpu.make_async_remote_copy(
            w_hbm.at[quarter(i), pl.ds(col, 512)], WG.at[yr, x, quarter(i)],
            w_ss.at[d - 1, yr], w_rs.at[d - 1, yr],
            device_id=(seq, y * 4 + xd), device_id_type=MESH)

    def w_share(d, yr, slot, sems, target):
        piece = WG.at[yr, (x + 4 - d) % 4, quarter(slot)]
        return pltpu.make_async_remote_copy(
            piece, piece, sems[0].at[d - 1, yr], sems[1].at[d - 1, yr],
            device_id=target, device_id_type=MESH)

    def w_arrived(d, yr):
        return w_share(d, yr, i, (w_ss, w_rs), (seq, y * 4 + (x + 4 - d) % 4))

    def w_cross(d, yr):
        return w_share(d, yr, i, (wy_ss, wy_rs), dev(z, y_mate))

    def w_crossed(d, yr):
        return w_share(d, yr, y_mate, (wy_ss, wy_rs), dev(z, y_mate))

    def w_chip(d, yr):
        return w_share(d, yr, i, (wf_ss, wf_rs), dev(z, chip_mate))

    def w_chipped(d, yr):
        return w_share(d, yr, chip_mate, (wf_ss, wf_rs), dev(z, chip_mate))

    def w_last(d, yr):
        return w_share(d, yr, y_mate, (wg_ss, wg_rs), dev(z, chip_mate))

    def w_lasted(d, yr):
        return w_share(d, yr, (chip_mate + 2) % 4, (wg_ss, wg_rs), dev(z, chip_mate))

    for d in (1, 3, 2):
        for yr in range(2):
            w_copy(d, yr).start()

    for h in range(HEADS):
        for a in range(3):
            loads[h][a].wait()
            source = QA[h] if a == 0 else KV[h, a - 1, ROWS:, :]
            TMP[a] = source.astype(f32)
            SM[h, a] = TMP[a, pl.ds(h, 256, stride=4), :].astype(bf16)
            SF[h, a] = TMP[a, pl.ds(4 * x + h, 64, stride=16), :].astype(bf16)

    def plane_copy(d, kind):
        s = plane_peer(d)
        return plane_descriptor(d, kind, s, i, s)

    def plane_arrived(d, kind):
        s = (i + 4 - d) % 4
        return plane_descriptor(d, kind, s, s, i)

    def plane_descriptor(d, kind, target, sender, slot):
        mid = pl.multiple_of(sender * 256, 256)
        far = pl.multiple_of(sender * 64, 64)
        src, dst = (
            (SF.at[slot, pl.ds(1, 2)], FKV.at[z, :, pl.ds(far, 64)]),
            (SF.at[slot, 0], FQ.at[pl.ds(far, 64)]),
            (SM.at[slot, pl.ds(1, 2)], KV.at[4, :, pl.ds(ROWS + mid, 256)]),
            (SM.at[slot, 0], QA.at[4, pl.ds(mid, 256)]),
        )[kind]
        return pltpu.make_async_remote_copy(
            src, dst, p_ss.at[d - 1, kind], p_rs.at[d - 1, kind],
            device_id=dev(z, target), device_id_type=MESH)

    def cross_query(s, sender):
        return pltpu.make_async_remote_copy(
            SM.at[s, 0], CQ.at[pl.ds(pl.multiple_of(sender * 256, 256), 256)],
            cq_ss.at[s], cq_rs.at[sender], device_id=dev(pair, s), device_id_type=MESH)

    for kind in (0, 1):
        for d in (2, 3, 1):
            plane_copy(d, kind).start()

    for kind in (2, 3):
        for d in (2, 3, 1):
            plane_copy(d, kind).start()

    @pl.when(zpar == 1)
    def _():
        for s in range(4):
            cross_query(s, i).start()

    own_mid = pl.multiple_of(i * 256, 256)
    own_far = pl.multiple_of(i * 64, 64)
    QA[4, pl.ds(own_mid, 256), :] = SM[i, 0]
    FQ[pl.ds(own_far, 64), :] = SF[i, 0]
    for a in range(2):
        KV[4, a, pl.ds(ROWS + own_mid, 256), :] = SM[i, 1 + a]
        FKV[z, a, pl.ds(own_far, 64), :] = SF[i, 1 + a]

    def forward(hop, slot):
        return pltpu.make_async_remote_copy(
            FKV.at[slot], FKV.at[slot], f_ss.at[hop], f_rs.at[hop],
            device_id=dev(znext, i), device_id_type=MESH)

    def backward(hop, slot):
        return pltpu.make_async_remote_copy(
            FKV.at[slot], FKV.at[slot], b_ss.at[hop], b_rs.at[hop],
            device_id=dev(zprev, i), device_id_type=MESH)

    def tiles(h, with_prev):
        for b in range(ROWS // TILE):
            rows = slice(b * TILE, (b + 1) * TILE)
            pieces = []
            if with_prev:
                pieces.append((KV[h, 0, :ROWS, :], KV[h, 1, :ROWS, :], None))
            if b:
                pieces.append((KV[h, 0, ROWS:ROWS + b * TILE, :], KV[h, 1, ROWS:ROWS + b * TILE, :], None))
            diag = slice(ROWS + b * TILE, ROWS + (b + 1) * TILE)
            pieces.append((KV[h, 0, diag, :], KV[h, 1, diag, :], 0))
            numer, peak, total = softmax_pieces(QA[h, rows, :], pieces)
            ACC[h, rows, :] = numer
            PK[h, rows, :] = peak
            TT[h, rows, :] = total

    def x_copy(part, sem):
        return (
            pltpu.make_async_remote_copy(
                AG.at[(0,) + part], AG.at[(1,) + part], ar_ss.at[sem], ar_rs.at[sem],
                device_id=right, device_id_type=MESH),
            pltpu.make_async_remote_copy(
                AG.at[(0,) + part], AG.at[(3,) + part], al_ss.at[sem], al_rs.at[sem],
                device_id=left, device_id_type=MESH),
        )

    def x_relay(part, sem):
        top = part + (pl.ds(0, 128),)
        low = part + (pl.ds(128, 128),)
        return (
            pltpu.make_async_remote_copy(
                AG.at[(1,) + top], AG.at[(2,) + top], or_ss.at[sem], or_rs.at[sem],
                device_id=right, device_id_type=MESH),
            pltpu.make_async_remote_copy(
                AG.at[(3,) + low], AG.at[(2,) + low], ol_ss.at[sem], ol_rs.at[sem],
                device_id=left, device_id_type=MESH),
        )

    def x_pass_on(part, sem):
        for arrived, onward in zip(x_copy(part, sem), x_relay(part, sem)):
            arrived.wait_recv()
            onward.start()

    def near_part(h):
        return (h, pl.ds(1, 3))

    def strided_part(h):
        return (h, 0)

    nfwd = planes // 2
    nbwd = planes - 1 - nfwd

    def level_step(h, carry):
        @pl.when((h < 4) & (core == 1))
        def _():
            for a in range(2):
                pltpu.make_async_remote_copy(
                    KV.at[h, a, pl.ds(0, ROWS)], KV.at[h, a, pl.ds(0, ROWS)], n_ss.at[h, a], n_rs.at[h, a],
                    device_id=dev(z, i + 1 - 2 * core), device_id_type=MESH).wait_recv()

        @pl.when(h == 4)
        def _():
            for kind in (2, 3):
                for d in (1, 2, 3):
                    plane_arrived(d, kind).wait_recv()

        parity = jnp.where(h < 4, core, 0)

        @pl.when(parity == 1)
        def _():
            tiles(h, True)

        @pl.when(parity == 0)
        def _():
            tiles(h, False)

        @pl.when(h == 0)
        def _():
            for kind in (0, 1):
                for d in (1, 2, 3):
                    plane_arrived(d, kind).wait_recv()

        @pl.when(h == 4)
        def _():
            for early in range(2):
                x_pass_on(near_part(early), early)

        @pl.when((h >= 1) & (h <= nfwd))
        def _():
            forward(h - 1, (z + planes - h) % planes).wait_recv()

        @pl.when((h >= 1) & (h <= nbwd))
        def _():
            backward(h - 1, (z + h) % planes).wait_recv()

        @pl.when(h < nfwd)
        def _():
            forward(h, (z + planes - h) % planes).start()

        @pl.when(h < nbwd)
        def _():
            backward(h, (z + h) % planes).start()

        @pl.when(h < 4)
        def _():
            for rr in range(1, 4):
                picked = (h, pl.ds((h + rr) % 4, 256, stride=4), slice(None))
                AG[0, h, rr] = (ACC[picked] / TT[picked]).astype(bf16)
            for copy in x_copy(near_part(h), h):
                copy.start()

        @pl.when(h == 1)
        def _():
            for d in (1, 3, 2):
                for yr in range(2):
                    w_arrived(d, yr).wait_recv()
                    w_cross(d, yr).start()
                    w_chip(d, yr).start()

        return carry

    lax.fori_loop(0, HEADS + 1, level_step, 0)

    lane = lax.broadcasted_iota(jnp.int32, (256, DH), 1)

    def pack(slot, numer, peak, total):
        OB[slot] = (numer / total).astype(bf16)
        ST[slot] = jnp.transpose(jnp.where(lane == 0, peak, total))[:8, :]

    def cross_result(s, sender, kind):
        src, dst = ((OB, RO), (ST, RST))[kind]
        return pltpu.make_async_remote_copy(
            src.at[4 + s], dst.at[4 + sender], cr_ss.at[s, kind], cr_rs.at[sender, kind],
            device_id=dev(pair, s), device_id_type=MESH)

    @pl.when(zpar == 0)
    def _():
        for s in range(4):
            cross_query(s, s).wait_recv()
            rows = slice(s * 256, (s + 1) * 256)
            pack(4 + s, *softmax_pieces(CQ[rows, :], [(KV[4, 0, ROWS:, :], KV[4, 1, ROWS:, :], None)]))
            for kind in range(2):
                cross_result(s, i, kind).start()

    far_pieces = [(FKV[j, 0], FKV[j, 1], TILE * (z - j)) for j in range(planes)]
    far = softmax_pieces(FQ[...], far_pieces)
    picked = (4, pl.ds(x, 256, stride=4), slice(None))
    mid = (ACC[picked], PK[picked], TT[picked])
    ACC[picked], PK[picked], TT[picked] = merge(mid, far)
    for s in range(4):
        rows = slice(s * 256, (s + 1) * 256)
        pack(s, ACC[4, rows, :], PK[4, rows, :], TT[4, rows, :])

    def back_copy(d, kind):
        s = plane_peer(d)
        src, dst = ((OB, RO), (ST, RST))[kind]
        return pltpu.make_async_remote_copy(
            src.at[s], dst.at[i], r_ss.at[d - 1, kind], r_rs.at[d - 1, kind],
            device_id=dev(z, s), device_id_type=MESH)

    def back_arrived(d, kind):
        s = (i + 4 - d) % 4
        src, dst = ((OB, RO), (ST, RST))[kind]
        return pltpu.make_async_remote_copy(
            src.at[i], dst.at[s], r_ss.at[d - 1, kind], r_rs.at[d - 1, kind],
            device_id=dev(z, s), device_id_type=MESH)

    for d in (2, 3, 1):
        for kind in range(2):
            back_copy(d, kind).start()
    RO[i] = OB[i]
    RST[i] = ST[i]

    for late in (2, 3):
        x_pass_on(near_part(late), late)

    for d in (1, 3, 2):
        for yr in range(2):
            w_crossed(d, yr).wait_recv()
            w_last(d, yr).start()

    for d in (1, 2, 3):
        for kind in range(2):
            back_arrived(d, kind).wait_recv()

    @pl.when(zpar == 1)
    def _():
        for s in range(4):
            for kind in range(2):
                cross_result(s, s, kind).wait_recv()

    def unpack(slot):
        stats = jnp.transpose(RST[slot])
        peak = jnp.broadcast_to(stats[:, 0:1], (256, DH))
        total = jnp.broadcast_to(stats[:, 1:2], (256, DH))
        return RO[slot].astype(f32) * total, peak, total

    for s in range(HEADS):
        picked = (s, pl.ds(s, 256, stride=4), slice(None))
        state = merge((ACC[picked], PK[picked], TT[picked]), unpack(s))

        @pl.when(zpar == 0)
        def _():
            AG[0, s, 0] = (state[0] / state[2]).astype(bf16)

        @pl.when(zpar == 1)
        def _():
            numer, _, total = merge(state, unpack(4 + s))
            AG[0, s, 0] = (numer / total).astype(bf16)

        for copy in x_copy(strided_part(s), 4 + s):
            copy.start()

    for d in (1, 2, 3):
        for yr in range(2):
            w_chipped(d, yr).wait_recv()
            w_lasted(d, yr).wait_recv()
    for yr in range(2):
        w_own(yr).wait()

    def weight(yr, j, h):
        return WG[yr, (x + 4 - j) % 4, h * DH:(h + 1) * DH, :]

    def product(r, yr, blocks):
        left_side = jnp.concatenate([AG[j, h, (r - h) % 4] for j, h in blocks], axis=1)
        right_side = jnp.concatenate([weight(yr, j, h) for j, h in blocks], axis=0)
        return jnp.dot(left_side, right_side, preferred_element_type=f32)

    for r in range(4):
        blocks = [(j, h) for j in (0, 1, 3) for h in range(HEADS) if h != r]
        for yr, acc in ((1, OTH), (0, OWN)):
            acc[r] = product(r, yr, blocks)

    def to_across(r):
        return pltpu.make_async_remote_copy(
            PS.at[r], PR.at[r], y_ss.at[r], y_rs.at[r], device_id=across, device_id_type=MESH)

    def finish(r):
        for copy in x_relay(strided_part(r), 4 + r):
            copy.wait_recv()
        blocks = [(2, h) for h in range(HEADS) if h != r] + [(j, r) for j in range(4)]
        PS[r] = (OTH[r] + product(r, 1, blocks)).astype(bf16)
        to_across(r).start()
        OWN[r] = OWN[r] + product(r, 0, blocks)

    for r in range(4):
        x_pass_on(strided_part(r), 4 + r)
        if r == 0:
            for h in range(HEADS):
                for copy in x_relay(near_part(h), h):
                    copy.wait_recv()
        else:
            finish(r - 1)
    finish(3)

    for r in range(4):
        to_across(r).wait_recv()
        mixed = OWN[r] + PR[r].astype(f32)
        for c in range(4):
            ACC[c, pl.ds(r, 256, stride=4), :] = mixed[:, c * DH:(c + 1) * DH]
    for c in range(4):
        out_ref[:, c * DH:(c + 1) * DH] = ACC[c].astype(bf16)

    for d in (1, 2, 3):
        for yr in range(2):
            w_copy(d, yr).wait_send()
            w_cross(d, yr).wait_send()
            w_chip(d, yr).wait_send()
            w_last(d, yr).wait_send()
        for kind in range(4):
            plane_copy(d, kind).wait_send()
        for kind in range(2):
            back_copy(d, kind).wait_send()
    for hop in range(nfwd):
        forward(hop, (z + planes - hop) % planes).wait_send()
    for hop in range(nbwd):
        backward(hop, (z + hop) % planes).wait_send()
    for h in range(HEADS):
        for part, sem in ((near_part(h), h), (strided_part(h), 4 + h)):
            for copy in x_copy(part, sem) + x_relay(part, sem):
                copy.wait_send()
        to_across(h).wait_send()

    @pl.when(zpar == 1)
    def _():
        for s in range(4):
            cross_query(s, i).wait_send()

    @pl.when(zpar == 0)
    def _():
        for s in range(4):
            for kind in range(2):
                cross_result(s, i, kind).wait_send()

    @pl.when(core == 0)
    def _():
        for h in range(HEADS):
            for a in range(2):
                near_copy(h, a).wait_send()


def shards(planes, queries, keys, values, out_weight):
    dma = pltpu.SemaphoreType.DMA
    vmem = pltpu.VMEM
    anywhere = pl.BlockSpec(memory_space=pltpu.HBM)
    return pl.pallas_call(
        functools.partial(layer_kernel, planes),
        name="layer",
        out_shape=jax.ShapeDtypeStruct((ROWS, HEADS * DH), bf16),
        in_specs=[anywhere] * 4,
        out_specs=pl.BlockSpec(memory_space=pltpu.VMEM),
        scratch_shapes=[
            vmem((5, ROWS, DH), bf16),
            vmem((5, 2, 2 * ROWS, DH), bf16),
            vmem((4, 3, 256, DH), bf16),
            vmem((4, 3, 64, DH), bf16),
            vmem((256, DH), bf16),
            vmem((planes, 2, 256, DH), bf16),
            vmem((5, ROWS, DH), f32),
            vmem((5, ROWS, DH), f32),
            vmem((5, ROWS, DH), f32),
            vmem((3, ROWS, DH), f32),
            vmem((8, 256, DH), bf16),
            vmem((8, 8, 256), f32),
            vmem((8, 256, DH), bf16),
            vmem((8, 8, 256), f32),
            vmem((ROWS, DH), bf16),
            vmem((2, 4, 512, 512), bf16),
            vmem((4, 4, 4, 256, DH), bf16),
            vmem((4, 256, 512), bf16),
            vmem((4, 256, 512), bf16),
            vmem((4, 256, 512), f32),
            vmem((4, 256, 512), f32),
            dma((4, 3)), dma((2,)),
            dma((3, 2)), dma((3, 2)), dma((3, 2)), dma((3, 2)),
            dma((3, 2)), dma((3, 2)), dma((3, 2)), dma((3, 2)),
            dma((4, 2)), dma((4, 2)),
            dma((3, 4)), dma((3, 4)),
            dma((4,)), dma((4,)),
            dma((4,)), dma((4,)), dma((4,)), dma((4,)),
            dma((3, 2)), dma((3, 2)),
            dma((4, 2)), dma((4, 2)),
        ] + [dma((8,))] * 8 + [dma((4,))] * 2,
        compiler_params=pltpu.CompilerParams(
            collective_id=0, has_side_effects=True, vmem_limit_bytes=52 * 1024 * 1024),
    )(queries, keys, values, out_weight)


def solution(mesh):
    placed = (P("seq", "head"), P("seq", "head"), P("seq", "head"), P("head", None))
    planes = mesh.shape["seq"] // 4
    return jax.shard_map(
        functools.partial(shards, planes), mesh=mesh, in_specs=placed, out_specs=P("seq", "head"), check_vma=False
    )
```

```python
import functools
import math

import jax
import jax.numpy as jnp
from jax import lax
from jax.experimental import pallas as pl
from jax.experimental.pallas import tpu as pltpu
from jax.sharding import PartitionSpec as P

DH = 128
ROWS = 1024
HEADS = 4
TILE = 256
NEG = -1e30
SCALE2 = math.log2(math.e) / math.sqrt(DH)
MESH = pl.DeviceIdType.MESH
bf16 = jnp.bfloat16
f32 = jnp.float32


def nt_dot(a, b):
    return lax.dot_general(a, b, (((1,), (1,)), ((), ())), preferred_element_type=f32)


def softmax_pieces(query, pieces):
    scores = []
    for key_rows, _, limit in pieces:
        score = nt_dot(query, key_rows)
        if limit is not None:
            row = lax.broadcasted_iota(jnp.int32, score.shape, 0)
            col = lax.broadcasted_iota(jnp.int32, score.shape, 1)
            score = jnp.where(col - row <= limit, score, NEG)
        scores.append(score)
    peak = functools.reduce(jnp.maximum, [jnp.max(s, axis=1, keepdims=True) for s in scores])
    both = None
    for score, (_, value_rows, _) in zip(scores, pieces):
        weights = jnp.exp2((score - peak) * SCALE2).astype(bf16)
        ones = jnp.ones(value_rows.shape, bf16)
        term = jnp.dot(weights, jnp.concatenate([value_rows, ones], axis=1), preferred_element_type=f32)
        both = term if both is None else both + term
    numer, total = both[:, :DH], both[:, DH:]
    return numer, jnp.broadcast_to(peak, numer.shape), total


def merge(one, two):
    numer1, peak1, total1 = one
    numer2, peak2, total2 = two
    top = jnp.maximum(peak1, peak2)
    f1 = jnp.exp2((peak1 - top) * SCALE2)
    f2 = jnp.exp2((peak2 - top) * SCALE2)
    return numer1 * f1 + numer2 * f2, top, total1 * f1 + total2 * f2


def layer_kernel(
    planes,
    q_hbm, k_hbm, v_hbm, w_hbm, out_ref,
    QA, KV, SM, SF, FQ, FKV, ACC, PK, TT, TMP, RO, RST, OB, ST, CQ, WG, AG, PS, PR, OWN, OTH,
    loc, locw, w_ss, w_rs, wy_ss, wy_rs, wf_ss, wf_rs, wg_ss, wg_rs, n_ss, n_rs, p_ss, p_rs, cq_ss, cq_rs,
    f_ss, f_rs, b_ss, b_rs, r_ss, r_rs, cr_ss, cr_rs,
    ar_ss, ar_rs, al_ss, al_rs, or_ss, or_rs, ol_ss, ol_rs, y_ss, y_rs,
):
    seq = lax.axis_index("seq")
    head = lax.axis_index("head")
    z = seq // 4
    i = seq % 4
    core = seq % 2
    zpar = z % 2
    x = head % 4
    y = head // 4

    def dev(plane, slot):
        return (plane * 4 + slot, head)

    def plane_peer(d):
        return (i + d) % 4

    pair = z + 1 - 2 * zpar
    znext = (z + 1) % planes
    zprev = (z + planes - 1) % planes
    zother = (z + planes - 1 + 2 * zpar) % planes

    loads = []
    for h in range(HEADS):
        cols = slice(h * DH, (h + 1) * DH)
        loads.append([
            pltpu.make_async_copy(q_hbm.at[:, cols], QA.at[h], loc.at[h, 0]),
            pltpu.make_async_copy(k_hbm.at[:, cols], KV.at[h, 0, pl.ds(ROWS, ROWS)], loc.at[h, 1]),
            pltpu.make_async_copy(v_hbm.at[:, cols], KV.at[h, 1, pl.ds(ROWS, ROWS)], loc.at[h, 2]),
        ])
        for copy in loads[-1]:
            copy.start()

    def w_own(yr):
        col = pl.multiple_of((((y + yr) % 2) * 4 + x) * 512, 512)
        return pltpu.make_async_copy(w_hbm.at[:, pl.ds(col, 512)], WG.at[yr, x], locw.at[yr])

    for yr in range(2):
        w_own(yr).start()

    barrier = pltpu.get_barrier_semaphore()
    greet = [dev(z, plane_peer(d)) for d in (1, 2, 3)]
    greet += [dev(pair, s) for s in range(4)]
    greet += [dev(zother, i)]
    greet += [(seq, y * 4 + (x + d) % 4) for d in (1, 2, 3)]
    right = (seq, y * 4 + (x + 1) % 4)
    left = (seq, y * 4 + (x + 3) % 4)
    across = (seq, (1 - y) * 4 + x)
    greet += [across]
    for target in greet:
        pl.semaphore_signal(barrier, inc=1, device_id=target, device_id_type=MESH)
    pl.semaphore_wait(barrier, len(greet))

    def near_copy(h, a):
        src = (k_hbm, v_hbm)[a].at[:, h * DH:(h + 1) * DH]
        return pltpu.make_async_remote_copy(
            src, KV.at[h, a, pl.ds(0, ROWS)], n_ss.at[h, a], n_rs.at[h, a],
            device_id=dev(z, i + 1 - 2 * core), device_id_type=MESH)

    @pl.when(core == 0)
    def _():
        for h in range(HEADS):
            for a in range(2):
                near_copy(h, a).start()

    chip_mate = i + 1 - 2 * core
    y_mate = (i + 2) % 4

    def quarter(slot):
        return pl.ds(pl.multiple_of(slot * 128, 128), 128)

    def w_copy(d, yr):
        xd = (x + d) % 4
        yd = (y + yr) % 2
        col = pl.multiple_of((yd * 4 + xd) * 512, 512)
        return pltpu.make_async_remote_copy(
            w_hbm.at[quarter(i), pl.ds(col, 512)], WG.at[yr, x, quarter(i)],
            w_ss.at[d - 1, yr], w_rs.at[d - 1, yr],
            device_id=(seq, y * 4 + xd), device_id_type=MESH)

    def w_share(d, yr, slot, sems, target):
        piece = WG.at[yr, (x + 4 - d) % 4, quarter(slot)]
        return pltpu.make_async_remote_copy(
            piece, piece, sems[0].at[d - 1, yr], sems[1].at[d - 1, yr],
            device_id=target, device_id_type=MESH)

    def w_arrived(d, yr):
        return w_share(d, yr, i, (w_ss, w_rs), (seq, y * 4 + (x + 4 - d) % 4))

    def w_cross(d, yr):
        return w_share(d, yr, i, (wy_ss, wy_rs), dev(z, y_mate))

    def w_crossed(d, yr):
        return w_share(d, yr, y_mate, (wy_ss, wy_rs), dev(z, y_mate))

    def w_chip(d, yr):
        return w_share(d, yr, i, (wf_ss, wf_rs), dev(z, chip_mate))

    def w_chipped(d, yr):
        return w_share(d, yr, chip_mate, (wf_ss, wf_rs), dev(z, chip_mate))

    def w_last(d, yr):
        return w_share(d, yr, y_mate, (wg_ss, wg_rs), dev(z, chip_mate))

    def w_lasted(d, yr):
        return w_share(d, yr, (chip_mate + 2) % 4, (wg_ss, wg_rs), dev(z, chip_mate))

    for d in (1, 3, 2):
        for yr in range(2):
            w_copy(d, yr).start()

    for h in range(HEADS):
        for a in range(3):
            loads[h][a].wait()
            source = QA[h] if a == 0 else KV[h, a - 1, ROWS:, :]
            TMP[a] = source.astype(f32)
            SM[h, a] = TMP[a, pl.ds(h, 256, stride=4), :].astype(bf16)
            SF[h, a] = TMP[a, pl.ds(4 * x + h, 64, stride=16), :].astype(bf16)

    def plane_copy(d, kind):
        s = plane_peer(d)
        return plane_descriptor(d, kind, s, i, s)

    def plane_arrived(d, kind):
        s = (i + 4 - d) % 4
        return plane_descriptor(d, kind, s, s, i)

    def plane_descriptor(d, kind, target, sender, slot):
        mid = pl.multiple_of(sender * 256, 256)
        far = pl.multiple_of(sender * 64, 64)
        src, dst = (
            (SF.at[slot, pl.ds(1, 2)], FKV.at[z, :, pl.ds(far, 64)]),
            (SF.at[slot, 0], FQ.at[pl.ds(far, 64)]),
            (SM.at[slot, pl.ds(1, 2)], KV.at[4, :, pl.ds(ROWS + mid, 256)]),
            (SM.at[slot, 0], QA.at[4, pl.ds(mid, 256)]),
        )[kind]
        return pltpu.make_async_remote_copy(
            src, dst, p_ss.at[d - 1, kind], p_rs.at[d - 1, kind],
            device_id=dev(z, target), device_id_type=MESH)

    def cross_query(s, sender):
        return pltpu.make_async_remote_copy(
            SM.at[s, 0], CQ.at[pl.ds(pl.multiple_of(sender * 256, 256), 256)],
            cq_ss.at[s], cq_rs.at[sender], device_id=dev(pair, s), device_id_type=MESH)

    for kind in (0, 1):
        for d in (2, 3, 1):
            plane_copy(d, kind).start()

    for kind in (2, 3):
        for d in (2, 3, 1):
            plane_copy(d, kind).start()

    @pl.when(zpar == 1)
    def _():
        for s in range(4):
            cross_query(s, i).start()

    own_mid = pl.multiple_of(i * 256, 256)
    own_far = pl.multiple_of(i * 64, 64)
    QA[4, pl.ds(own_mid, 256), :] = SM[i, 0]
    FQ[pl.ds(own_far, 64), :] = SF[i, 0]
    for a in range(2):
        KV[4, a, pl.ds(ROWS + own_mid, 256), :] = SM[i, 1 + a]
        FKV[z, a, pl.ds(own_far, 64), :] = SF[i, 1 + a]

    def forward(hop, slot):
        return pltpu.make_async_remote_copy(
            FKV.at[slot], FKV.at[slot], f_ss.at[hop], f_rs.at[hop],
            device_id=dev(znext, i), device_id_type=MESH)

    def backward(hop, slot):
        return pltpu.make_async_remote_copy(
            FKV.at[slot], FKV.at[slot], b_ss.at[hop], b_rs.at[hop],
            device_id=dev(zprev, i), device_id_type=MESH)

    def tiles(h, with_prev):
        for b in range(ROWS // TILE):
            rows = slice(b * TILE, (b + 1) * TILE)
            pieces = []
            if with_prev:
                pieces.append((KV[h, 0, :ROWS, :], KV[h, 1, :ROWS, :], None))
            if b:
                pieces.append((KV[h, 0, ROWS:ROWS + b * TILE, :], KV[h, 1, ROWS:ROWS + b * TILE, :], None))
            diag = slice(ROWS + b * TILE, ROWS + (b + 1) * TILE)
            pieces.append((KV[h, 0, diag, :], KV[h, 1, diag, :], 0))
            numer, peak, total = softmax_pieces(QA[h, rows, :], pieces)
            ACC[h, rows, :] = numer
            PK[h, rows, :] = peak
            TT[h, rows, :] = total

    def x_copy(part, sem):
        return (
            pltpu.make_async_remote_copy(
                AG.at[(0,) + part], AG.at[(1,) + part], ar_ss.at[sem], ar_rs.at[sem],
                device_id=right, device_id_type=MESH),
            pltpu.make_async_remote_copy(
                AG.at[(0,) + part], AG.at[(3,) + part], al_ss.at[sem], al_rs.at[sem],
                device_id=left, device_id_type=MESH),
        )

    def x_relay(part, sem):
        top = part + (pl.ds(0, 128),)
        low = part + (pl.ds(128, 128),)
        return (
            pltpu.make_async_remote_copy(
                AG.at[(1,) + top], AG.at[(2,) + top], or_ss.at[sem], or_rs.at[sem],
                device_id=right, device_id_type=MESH),
            pltpu.make_async_remote_copy(
                AG.at[(3,) + low], AG.at[(2,) + low], ol_ss.at[sem], ol_rs.at[sem],
                device_id=left, device_id_type=MESH),
        )

    def x_pass_on(part, sem):
        for arrived, onward in zip(x_copy(part, sem), x_relay(part, sem)):
            arrived.wait_recv()
            onward.start()

    def near_part(h):
        return (h, pl.ds(1, 3))

    def strided_part(h):
        return (h, 0)

    nfwd = planes // 2
    nbwd = planes - 1 - nfwd

    def level_step(h, carry):
        @pl.when((h < 4) & (core == 1))
        def _():
            for a in range(2):
                pltpu.make_async_remote_copy(
                    KV.at[h, a, pl.ds(0, ROWS)], KV.at[h, a, pl.ds(0, ROWS)], n_ss.at[h, a], n_rs.at[h, a],
                    device_id=dev(z, i + 1 - 2 * core), device_id_type=MESH).wait_recv()

        @pl.when(h == 4)
        def _():
            for kind in (2, 3):
                for d in (1, 2, 3):
                    plane_arrived(d, kind).wait_recv()

        parity = jnp.where(h < 4, core, 0)

        @pl.when(parity == 1)
        def _():
            tiles(h, True)

        @pl.when(parity == 0)
        def _():
            tiles(h, False)

        @pl.when(h == 0)
        def _():
            for kind in (0, 1):
                for d in (1, 2, 3):
                    plane_arrived(d, kind).wait_recv()

        @pl.when(h == 4)
        def _():
            for early in range(2):
                x_pass_on(near_part(early), early)

        @pl.when((h >= 1) & (h <= nfwd))
        def _():
            forward(h - 1, (z + planes - h) % planes).wait_recv()

        @pl.when((h >= 1) & (h <= nbwd))
        def _():
            backward(h - 1, (z + h) % planes).wait_recv()

        @pl.when(h < nfwd)
        def _():
            forward(h, (z + planes - h) % planes).start()

        @pl.when(h < nbwd)
        def _():
            backward(h, (z + h) % planes).start()

        @pl.when(h < 4)
        def _():
            for rr in range(1, 4):
                picked = (h, pl.ds((h + rr) % 4, 256, stride=4), slice(None))
                AG[0, h, rr] = (ACC[picked] / TT[picked]).astype(bf16)
            for copy in x_copy(near_part(h), h):
                copy.start()

        @pl.when(h == 1)
        def _():
            for d in (1, 3, 2):
                for yr in range(2):
                    w_arrived(d, yr).wait_recv()
                    w_cross(d, yr).start()
                    w_chip(d, yr).start()

        return carry

    lax.fori_loop(0, HEADS + 1, level_step, 0)

    lane = lax.broadcasted_iota(jnp.int32, (256, DH), 1)

    def pack(slot, numer, peak, total):
        OB[slot] = (numer / total).astype(bf16)
        ST[slot] = jnp.transpose(jnp.where(lane == 0, peak, total))[:8, :]

    def cross_result(s, sender, kind):
        src, dst = ((OB, RO), (ST, RST))[kind]
        return pltpu.make_async_remote_copy(
            src.at[4 + s], dst.at[4 + sender], cr_ss.at[s, kind], cr_rs.at[sender, kind],
            device_id=dev(pair, s), device_id_type=MESH)

    @pl.when(zpar == 0)
    def _():
        for s in range(4):
            cross_query(s, s).wait_recv()
            rows = slice(s * 256, (s + 1) * 256)
            pack(4 + s, *softmax_pieces(CQ[rows, :], [(KV[4, 0, ROWS:, :], KV[4, 1, ROWS:, :], None)]))
            for kind in range(2):
                cross_result(s, i, kind).start()

    far_pieces = [(FKV[j, 0], FKV[j, 1], TILE * (z - j)) for j in range(planes)]
    far = softmax_pieces(FQ[...], far_pieces)
    picked = (4, pl.ds(x, 256, stride=4), slice(None))
    mid = (ACC[picked], PK[picked], TT[picked])
    ACC[picked], PK[picked], TT[picked] = merge(mid, far)
    for s in range(4):
        rows = slice(s * 256, (s + 1) * 256)
        pack(s, ACC[4, rows, :], PK[4, rows, :], TT[4, rows, :])

    def back_copy(d, kind):
        s = plane_peer(d)
        src, dst = ((OB, RO), (ST, RST))[kind]
        return pltpu.make_async_remote_copy(
            src.at[s], dst.at[i], r_ss.at[d - 1, kind], r_rs.at[d - 1, kind],
            device_id=dev(z, s), device_id_type=MESH)

    def back_arrived(d, kind):
        s = (i + 4 - d) % 4
        src, dst = ((OB, RO), (ST, RST))[kind]
        return pltpu.make_async_remote_copy(
            src.at[i], dst.at[s], r_ss.at[d - 1, kind], r_rs.at[d - 1, kind],
            device_id=dev(z, s), device_id_type=MESH)

    for d in (2, 3, 1):
        for kind in range(2):
            back_copy(d, kind).start()
    RO[i] = OB[i]
    RST[i] = ST[i]

    for late in (2, 3):
        x_pass_on(near_part(late), late)

    for d in (1, 3, 2):
        for yr in range(2):
            w_crossed(d, yr).wait_recv()
            w_last(d, yr).start()

    for d in (1, 2, 3):
        for kind in range(2):
            back_arrived(d, kind).wait_recv()

    @pl.when(zpar == 1)
    def _():
        for s in range(4):
            for kind in range(2):
                cross_result(s, s, kind).wait_recv()

    def unpack(slot):
        stats = jnp.transpose(RST[slot])
        peak = jnp.broadcast_to(stats[:, 0:1], (256, DH))
        total = jnp.broadcast_to(stats[:, 1:2], (256, DH))
        return RO[slot].astype(f32) * total, peak, total

    for s in range(HEADS):
        picked = (s, pl.ds(s, 256, stride=4), slice(None))
        state = merge((ACC[picked], PK[picked], TT[picked]), unpack(s))

        @pl.when(zpar == 0)
        def _():
            AG[0, s, 0] = (state[0] / state[2]).astype(bf16)

        @pl.when(zpar == 1)
        def _():
            numer, _, total = merge(state, unpack(4 + s))
            AG[0, s, 0] = (numer / total).astype(bf16)

        for copy in x_copy(strided_part(s), 4 + s):
            copy.start()

    def weight(yr, j, h):
        return WG[yr, (x + 4 - j) % 4, h * DH:(h + 1) * DH, :]

    def product(r, yr, blocks):
        left_side = jnp.concatenate([AG[j, h, (r - h) % 4] for j, h in blocks], axis=1)
        right_side = jnp.concatenate([weight(yr, j, h) for j, h in blocks], axis=0)
        return jnp.dot(left_side, right_side, preferred_element_type=f32)

    def to_across(r):
        return pltpu.make_async_remote_copy(
            PS.at[r], PR.at[r], y_ss.at[r], y_rs.at[r], device_id=across, device_id_type=MESH)

    def finish(r):
        for copy in x_relay(strided_part(r), 4 + r):
            copy.wait_recv()
        blocks = [(2, h) for h in range(HEADS) if h != r] + [(j, r) for j in range(4)]
        PS[r] = (OTH[r] + product(r, 1, blocks)).astype(bf16)
        to_across(r).start()
        OWN[r] = OWN[r] + product(r, 0, blocks)

    def begin(r):
        blocks = [(j, h) for j in (0, 1, 3) for h in range(HEADS) if h != r]
        for yr, acc in ((1, OTH), (0, OWN)):
            acc[r] = product(r, yr, blocks)

    for d in (1, 2, 3):
        for yr in range(2):
            w_chipped(d, yr).wait_recv()
            w_lasted(d, yr).wait_recv()
    for yr in range(2):
        w_own(yr).wait()

    begin(0)
    for r in range(4):
        x_pass_on(strided_part(r), 4 + r)
        if r == 0:
            for h in range(HEADS):
                for copy in x_relay(near_part(h), h):
                    copy.wait_recv()
        else:
            finish(r - 1)
        if r < 3:
            begin(r + 1)
    finish(3)

    for r in range(4):
        to_across(r).wait_recv()
        mixed = OWN[r] + PR[r].astype(f32)
        for c in range(4):
            ACC[c, pl.ds(r, 256, stride=4), :] = mixed[:, c * DH:(c + 1) * DH]
    for c in range(4):
        out_ref[:, c * DH:(c + 1) * DH] = ACC[c].astype(bf16)

    for d in (1, 2, 3):
        for yr in range(2):
            w_copy(d, yr).wait_send()
            w_cross(d, yr).wait_send()
            w_chip(d, yr).wait_send()
            w_last(d, yr).wait_send()
        for kind in range(4):
            plane_copy(d, kind).wait_send()
        for kind in range(2):
            back_copy(d, kind).wait_send()
    for hop in range(nfwd):
        forward(hop, (z + planes - hop) % planes).wait_send()
    for hop in range(nbwd):
        backward(hop, (z + hop) % planes).wait_send()
    for h in range(HEADS):
        for part, sem in ((near_part(h), h), (strided_part(h), 4 + h)):
            for copy in x_copy(part, sem) + x_relay(part, sem):
                copy.wait_send()
        to_across(h).wait_send()

    @pl.when(zpar == 1)
    def _():
        for s in range(4):
            cross_query(s, i).wait_send()

    @pl.when(zpar == 0)
    def _():
        for s in range(4):
            for kind in range(2):
                cross_result(s, i, kind).wait_send()

    @pl.when(core == 0)
    def _():
        for h in range(HEADS):
            for a in range(2):
                near_copy(h, a).wait_send()


def shards(planes, queries, keys, values, out_weight):
    dma = pltpu.SemaphoreType.DMA
    vmem = pltpu.VMEM
    anywhere = pl.BlockSpec(memory_space=pltpu.HBM)
    return pl.pallas_call(
        functools.partial(layer_kernel, planes),
        name="layer",
        out_shape=jax.ShapeDtypeStruct((ROWS, HEADS * DH), bf16),
        in_specs=[anywhere] * 4,
        out_specs=pl.BlockSpec(memory_space=pltpu.VMEM),
        scratch_shapes=[
            vmem((5, ROWS, DH), bf16),
            vmem((5, 2, 2 * ROWS, DH), bf16),
            vmem((4, 3, 256, DH), bf16),
            vmem((4, 3, 64, DH), bf16),
            vmem((256, DH), bf16),
            vmem((planes, 2, 256, DH), bf16),
            vmem((5, ROWS, DH), f32),
            vmem((5, ROWS, DH), f32),
            vmem((5, ROWS, DH), f32),
            vmem((3, ROWS, DH), f32),
            vmem((8, 256, DH), bf16),
            vmem((8, 8, 256), f32),
            vmem((8, 256, DH), bf16),
            vmem((8, 8, 256), f32),
            vmem((ROWS, DH), bf16),
            vmem((2, 4, 512, 512), bf16),
            vmem((4, 4, 4, 256, DH), bf16),
            vmem((4, 256, 512), bf16),
            vmem((4, 256, 512), bf16),
            vmem((4, 256, 512), f32),
            vmem((4, 256, 512), f32),
            dma((4, 3)), dma((2,)),
            dma((3, 2)), dma((3, 2)), dma((3, 2)), dma((3, 2)),
            dma((3, 2)), dma((3, 2)), dma((3, 2)), dma((3, 2)),
            dma((4, 2)), dma((4, 2)),
            dma((3, 4)), dma((3, 4)),
            dma((4,)), dma((4,)),
            dma((4,)), dma((4,)), dma((4,)), dma((4,)),
            dma((3, 2)), dma((3, 2)),
            dma((4, 2)), dma((4, 2)),
        ] + [dma((8,))] * 8 + [dma((4,))] * 2,
        compiler_params=pltpu.CompilerParams(
            collective_id=0, has_side_effects=True, vmem_limit_bytes=52 * 1024 * 1024),
    )(queries, keys, values, out_weight)


def solution(mesh):
    placed = (P("seq", "head"), P("seq", "head"), P("seq", "head"), P("head", None))
    planes = mesh.shape["seq"] // 4
    return jax.shard_map(
        functools.partial(shards, planes), mesh=mesh, in_specs=placed, out_specs=P("seq", "head"), check_vma=False
    )
```
